128 devices in a mesh: row: 8 (over y, core), col: 16 (over x, z).
Axes of the slice: x: 4, y: 4, z: 4, core: 2. Of those that a mesh axis runs over, the one named last changes fastest.
Arguments:
- scores: float32 [32, 98304], P(None, ('row', 'col')), may hold values from -60 to 60
- tile_values: bfloat16 [8, 16, 480, 128, 128], P('row', 'col'), may hold values from 0 to 1
- tile_rows: int32 [8, 16, 480], P('row', 'col'), may hold values from 0 to 95, as said below
- tile_cols: int32 [8, 16, 480], P('row', 'col'), may hold values from 0 to 47, as said below
- tile_count: int32 [8, 16], P('row', 'col'), may hold values from 240 to 480, as said below
Outputs:
- solution: float32 [32, 98304], P(None, ('row', 'col'))
- residual: float32 [32, 98304], P(None, ('row', 'col'))
The draws below stay inside these ranges and needn't reach their ends.
Inputs may be any that keep to these rules, and one draw needn't show every extreme that they name: `tile_rows`: on every device each local row tile is named by exactly 5 of the 480 slots. `tile_cols`: on every device each local column tile is named by exactly 10 of the slots. Only the first tile_count slots of a device are live; some device has all 480 slots live.
All inputs are finite; a program needn't handle non-finite values.
Results may differ from the reference program's by a relative error of at most 0.0031.
Values may be sent and summed in bfloat16 or wider, within the bound.
A program may use at most 128 MiB of HBM per device.

```python
import math
import jax
import jax.numpy as jnp
from jax import lax

TASKS = 32
TILE = 128
PER_ROW = 5
TPB = 6
ITERS = 3
DOCS = 98304
ROW_TILES = 96
COL_TILES = 48
SLOTS = 480
N_ROW = 8
N_COL = 16


def tile_lists(key):
    device_keys = jax.random.split(jax.random.fold_in(key, 11), N_ROW * N_COL)

    def one_device(device_key):
        first_key, second_key = jax.random.split(device_key)
        row_ids = jax.random.permutation(first_key, SLOTS) % ROW_TILES
        col_ids = jax.random.permutation(second_key, SLOTS) % COL_TILES
        return (row_ids.astype(jnp.int32), col_ids.astype(jnp.int32))
    row_ids, col_ids = jax.vmap(one_device)(device_keys)
    return (row_ids.reshape(N_ROW, N_COL, SLOTS), col_ids.reshape(N_ROW, N_COL, SLOTS))


def draw_tile_rows(key, part):
    return tile_lists(key)[0]


def draw_tile_cols(key, part):
    return tile_lists(key)[1]


def draw_tile_count(key, part):
    counts = jax.random.randint(jax.random.fold_in(key, 23), (N_ROW * N_COL,), SLOTS // 2, SLOTS + 1)
    full_device = jax.random.randint(jax.random.fold_in(key, 29), (), 0, N_ROW * N_COL)
    counts = counts.at[full_device].set(SLOTS)
    return counts.astype(jnp.int32).reshape(N_ROW, N_COL)


def draw_tile_values(key, part):
    density = 16.0 / (PER_ROW * N_COL * TILE)
    uniform_part = jax.random.uniform(jax.random.fold_in(key, 37), (N_ROW, N_COL, SLOTS, TILE, TILE), jnp.float32)
    lowest = 0.25
    weights = lowest + (1.0 - lowest) * (uniform_part / density)
    chosen = jnp.where(uniform_part < density, weights, 0.0)
    return chosen.astype(jnp.bfloat16)


def draw_scores(key, part):
    first_key, second_key = jax.random.split(jax.random.fold_in(key, 5))
    task_scale = jnp.exp(jax.random.uniform(first_key, (TASKS, 1), jnp.float32, math.log(0.3), math.log(3.0)))
    doc_scale = jnp.exp(math.log(3.0) * jnp.arange(DOCS, dtype=jnp.float32) / (DOCS - 1))[None, :]
    base_values = jnp.clip(jax.random.normal(second_key, (TASKS, DOCS), jnp.float32), -6.0, 6.0)
    return (base_values * task_scale * doc_scale).astype(jnp.float32)


def setup_inputs(seed: int = 0) -> dict:
    arg_keys = jax.random.split(jax.random.key(seed), 6)
    return {
        "scores": draw_scores(jax.random.fold_in(arg_keys[5], 71), 0),
        "tile_values": draw_tile_values(jax.random.fold_in(arg_keys[5], 71), 0),
        "tile_rows": draw_tile_rows(jax.random.fold_in(arg_keys[5], 71), 0),
        "tile_cols": draw_tile_cols(jax.random.fold_in(arg_keys[5], 71), 0),
        "tile_count": draw_tile_count(jax.random.fold_in(arg_keys[5], 71), 0),
    }


coupling = 0.2


def tile_products(field, tile_values, tile_rows, tile_cols, tile_count):
    field_rows = field.shape[0]
    blocks = field.astype(jnp.bfloat16).reshape(field_rows, DOCS // TILE, TILE)
    dev_tiles = tile_values.reshape(N_ROW * N_COL, SLOTS, TILE, TILE)
    local_rows = tile_rows.reshape(N_ROW * N_COL, SLOTS)
    local_cols = tile_cols.reshape(N_ROW * N_COL, SLOTS)
    live_counts = tile_count.reshape(N_ROW * N_COL)
    device_ids = jnp.arange(N_ROW * N_COL, dtype=jnp.int32)

    def one_device(running, device_item):
        forward_sum, backward_sum = running
        tiles_here, rows_here, cols_here, live_count, device_id = device_item
        row_block = device_id // N_COL
        col_block = device_id % N_COL
        global_rows = (row_block * ROW_TILES + rows_here).astype(jnp.int32)
        global_cols = (((cols_here // TPB) * N_COL + col_block) * TPB + cols_here % TPB).astype(jnp.int32)
        live_mask = (jnp.arange(SLOTS, dtype=jnp.int32) < live_count).astype(jnp.float32)
        wide_tiles = tiles_here.astype(jnp.float32)
        col_pieces = jnp.take(blocks, global_cols, axis=1).astype(jnp.float32)
        row_pieces = jnp.take(blocks, global_rows, axis=1).astype(jnp.float32)
        forward = jnp.einsum("ksd,sod->kso", col_pieces, wide_tiles) * live_mask[None, :, None]
        backward = jnp.einsum("kso,sod->ksd", row_pieces, wide_tiles) * live_mask[None, :, None]
        forward_sum = forward_sum.at[:, global_rows, :].add(forward)
        backward_sum = backward_sum.at[:, global_cols, :].add(backward)
        return (forward_sum, backward_sum), None

    empty_sum = jnp.zeros((field_rows, DOCS // TILE, TILE), jnp.float32)
    summed, unused = lax.scan(one_device, (empty_sum, empty_sum), (dev_tiles, local_rows, local_cols, live_counts, device_ids))
    forward_sum, backward_sum = summed
    return (0.5 * (forward_sum + backward_sum)).reshape(field_rows, DOCS)


def reference(scores, tile_values, tile_rows, tile_cols, tile_count):
    degree = tile_products(jnp.ones((1, DOCS), jnp.float32), tile_values, tile_rows, tile_cols, tile_count)

    def operate(direction):
        graph_part = tile_products(direction, tile_values, tile_rows, tile_cols, tile_count)
        return direction + coupling * (degree * direction - graph_part)

    solution = jnp.zeros_like(scores)
    residual = scores
    direction = scores
    norm_now = jnp.sum(residual * residual, axis=1)
    for step_index in range(ITERS):
        image_field = operate(direction)
        step_size = norm_now / jnp.sum(direction * image_field, axis=1)
        solution = solution + step_size[:, None] * direction
        residual = residual - step_size[:, None] * image_field
        norm_next = jnp.sum(residual * residual, axis=1)
        direction = residual + (norm_next / norm_now)[:, None] * direction
        norm_now = norm_next
    return solution, residual
```

```python
import functools

import jax
import jax.numpy as jnp
from jax import lax
from jax.experimental import pallas as pl
from jax.experimental.pallas import tpu as pltpu
from jax.sharding import PartitionSpec as P

PER_ROW = 5
ITERS = 3
MESH = pl.DeviceIdType.MESH
SUM_TYPE = jnp.float32

coupling = 0.2


def spread(n):
    fast = 2 if n <= 8 else 4
    return n // fast, fast


def partner(me, k, n):
    slow, fast = spread(n)
    a = lax.rem(me // fast + slow // 2 + k // fast, slow)
    b = lax.rem(lax.rem(me, fast) + fast // 2 + lax.rem(k, fast), fast)
    return a * fast + b


def own_turn(n):
    slow, fast = spread(n)
    return (slow - slow // 2) % slow * fast + (fast - fast // 2) % fast


def cg_kernel(
    n_row, n_col, per_col,
    row_table, col_table, scores, tiles_hbm, sol, res,
    tiles, x_col, x_row, f_part, b_part, f_recv, b_recv,
    df_part, db_part, df_recv, db_recv, ones, dir_ref, degree, dots_row, dots_col,
    tile_sem,
    agr_send, agr_recv, agc_send, agc_recv,
    rsf_send, rsf_recv, rsb_send, rsb_recv,
    dgf_send, dgf_recv, dgb_send, dgb_recv,
    d1_send, d1_recv, d2_send, d2_recv,
):
    me_r = lax.axis_index("row")
    me_c = lax.axis_index("col")
    tasks = scores.shape[0]
    own_tiles = scores.shape[1] // 128
    slots = tiles.shape[0]
    col_tiles = b_part.shape[0]
    row_tiles = f_part.shape[0]
    chunk = slots // tile_sem.shape[0]

    def tile_copy(i):
        part = pl.ds(i * chunk, chunk)
        return pltpu.make_async_copy(tiles_hbm.at[part], tiles.at[part], tile_sem.at[i])

    for i in range(tile_sem.shape[0]):
        tile_copy(i).start()

    barrier = pltpu.get_barrier_semaphore()

    def greet(axis, n, own):
        def one(k, carry):
            @pl.when(k != own_turn(n))
            def _():
                j = partner(own, k, n)
                target = (me_r, j) if axis == "col" else (j, me_c)
                pl.semaphore_signal(barrier, inc=1, device_id=target, device_id_type=MESH)
            return carry

        lax.fori_loop(0, n, one, 0)

    greet("col", n_col, me_c)
    greet("row", n_row, me_r)

    x_col[col_tiles] = jnp.zeros((tasks, 128), jnp.bfloat16)
    x_row[row_tiles] = jnp.zeros((tasks, 128), jnp.bfloat16)
    ones[0] = jnp.ones((16, 128), jnp.bfloat16)
    ones[1] = jnp.zeros((16, 128), jnp.bfloat16)
    dir_ref[...] = scores[...]
    res[...] = scores[...]
    sol[...] = jnp.zeros_like(sol)

    pl.semaphore_wait(barrier, n_row + n_col - 2)

    def each_partner(n, own, action):
        def one(k, carry):
            @pl.when(k != own_turn(n))
            def _():
                action(partner(own, k, n))
            return carry

        lax.fori_loop(0, n, one, 0)

    own_col = pl.ds(me_r * own_tiles, own_tiles)
    own_row = pl.ds(me_c * own_tiles, own_tiles)

    def gather_row(j, source):
        part = pl.ds(source * own_tiles, own_tiles)
        return pltpu.make_async_remote_copy(
            src_ref=x_col.at[part], dst_ref=x_col.at[part],
            send_sem=agr_send.at[j], recv_sem=agr_recv.at[source],
            device_id=(j, me_c), device_id_type=MESH,
        )

    def gather_col(j, source):
        part = pl.ds(source * own_tiles, own_tiles)
        return pltpu.make_async_remote_copy(
            src_ref=x_row.at[part], dst_ref=x_row.at[part],
            send_sem=agc_send.at[j], recv_sem=agc_recv.at[source],
            device_id=(me_r, j), device_id_type=MESH,
        )

    def send_pieces(j, source, part, recv, send_sem, recv_sem, axis):
        return pltpu.make_async_remote_copy(
            src_ref=part, dst_ref=recv.at[source],
            send_sem=send_sem.at[j], recv_sem=recv_sem.at[source],
            device_id=(me_r, j) if axis == "col" else (j, me_c), device_id_type=MESH,
        )

    def f_send(j, source):
        return send_pieces(
            j, source, f_part.at[pl.ds(j * own_tiles, own_tiles)], f_recv, rsf_send, rsf_recv, "col")

    def b_send(j, source):
        return send_pieces(
            j, source, b_part.at[pl.ds(j * own_tiles, own_tiles)], b_recv, rsb_send, rsb_recv, "row")

    def df_send(j, source):
        return send_pieces(j, source, df_part.at[j], df_recv, dgf_send, dgf_recv, "col")

    def db_send(j, source):
        return send_pieces(j, source, db_part.at[j], db_recv, dgb_send, dgb_recv, "row")

    def d1_copy(j, source):
        return send_pieces(j, source, dots_row.at[me_r], dots_row, d1_send, d1_recv, "row")

    def d2_copy(j, source):
        return send_pieces(j, source, dots_col.at[me_c], dots_col, d2_send, d2_recv, "col")

    def start_gather():
        for t in range(own_tiles):
            piece = dir_ref[:, 128 * t : 128 * (t + 1)].astype(jnp.bfloat16)
            x_col[me_r * own_tiles + t] = piece
            x_row[me_c * own_tiles + t] = piece
        each_partner(n_row, me_r, lambda j: gather_row(j, me_r).start())
        each_partner(n_col, me_c, lambda j: gather_col(j, me_c).start())

    def forward_tile(row, weigh):
        fields, weights = [], []
        for i in range(PER_ROW):
            code = row_table[row * PER_ROW + i]
            fields.append(weigh(x_col, code & 63, col_tiles))
            weights.append(tiles[code >> 6])
        return lax.dot_general(
            jnp.concatenate(fields, axis=1), jnp.concatenate(weights, axis=1),
            (((1,), (1,)), ((), ())), preferred_element_type=jnp.float32)

    def backward_tile(col, weigh):
        fields, weights = [], []
        for i in range(per_col):
            code = col_table[col * per_col + i]
            fields.append(weigh(x_row, code & 127, row_tiles))
            weights.append(tiles[code >> 7])
        return jnp.dot(
            jnp.concatenate(fields, axis=1), jnp.concatenate(weights, axis=0),
            preferred_element_type=jnp.float32)

    def field_of(x_ref, index, limit):
        return x_ref[index]

    def ones_of(x_ref, index, limit):
        return ones[jnp.where(index == limit, 1, 0)]

    start_gather()
    for i in range(tile_sem.shape[0]):
        tile_copy(i).wait()

    def degree_group(n, own, tile_of, part, send):
        def one(k, carry):
            j = partner(own, k, n)
            for t in range(own_tiles):
                part[j, t : t + 1, :] = tile_of(j * own_tiles + t, ones_of)[0:1]
            part[j, own_tiles:, :] = jnp.zeros((8 - own_tiles, 128), jnp.float32)

            @pl.when(k != own_turn(n))
            def _():
                send(j, own).start()
            return carry

        lax.fori_loop(0, n, one, 0)

    degree_group(n_col, me_c, forward_tile, df_part, df_send)
    degree_group(n_row, me_r, backward_tile, db_part, db_send)

    def product_group(n, own, tile_of, part, send):
        def one(k, carry):
            j = partner(own, k, n)
            for t in range(own_tiles):
                part[j * own_tiles + t] = tile_of(j * own_tiles + t, field_of).astype(part.dtype)

            @pl.when(k != own_turn(n))
            def _():
                send(j, own).start()
            return carry

        lax.fori_loop(0, n, one, 0)

    def gather_sums(n, own, send, recv, totals):
        def one(k, sums):
            j = lax.rem(own + 1 + k, n)
            send(j, j).wait_recv()
            return tuple(s + recv[j, t].astype(jnp.float32) for t, s in enumerate(sums))

        return lax.fori_loop(0, n - 1, one, totals)

    lane = lax.broadcasted_iota(jnp.int32, (tasks, 128), 1)
    task = lax.broadcasted_iota(jnp.int32, (tasks, 128), 0)

    def one_step(step, carry):
        each_partner(n_row, me_r, lambda j: gather_row(j, j).wait_recv())
        product_group(n_col, me_c, forward_tile, f_part, f_send)
        each_partner(n_col, me_c, lambda j: gather_col(j, j).wait_recv())
        product_group(n_row, me_r, backward_tile, b_part, b_send)

        @pl.when(step == 0)
        def _():
            total = df_part[me_c] + db_part[me_r]
            def add_f(k, t):
                j = lax.rem(me_c + 1 + k, n_col)
                df_send(j, j).wait_recv()
                return t + df_recv[j]
            def add_b(k, t):
                j = lax.rem(me_r + 1 + k, n_row)
                db_send(j, j).wait_recv()
                return t + db_recv[j]
            total = lax.fori_loop(0, n_col - 1, add_f, total)
            total = lax.fori_loop(0, n_row - 1, add_b, total)
            degree[...] = 0.5 * total
            each_partner(n_col, me_c, lambda j: df_send(j, me_c).wait_send())
            each_partner(n_row, me_r, lambda j: db_send(j, me_r).wait_send())

        totals = tuple(
            f_part[me_c * own_tiles + t].astype(jnp.float32)
            + b_part[me_r * own_tiles + t].astype(jnp.float32)
            for t in range(own_tiles))
        totals = gather_sums(n_row, me_r, b_send, b_recv, totals)
        totals = gather_sums(n_col, me_c, f_send, f_recv, totals)

        pq = jnp.zeros((tasks, 128), jnp.float32)
        rq, qq, rr = pq, pq, pq
        images = []
        for t in range(own_tiles):
            part = slice(128 * t, 128 * (t + 1))
            p, r = dir_ref[:, part], res[:, part]
            q = p + coupling * (degree[t : t + 1, :] * p - 0.5 * totals[t])
            images.append(q)
            pq, rq, qq, rr = pq + p * q, rq + r * q, qq + q * q, rr + r * r
        row = jnp.zeros((tasks, 128), jnp.float32)
        for i, s in enumerate((pq, rq, qq, rr)):
            row = jnp.where(lane == task + tasks * i, jnp.sum(s, axis=1, keepdims=True), row)
        row = jnp.sum(row, axis=0, keepdims=True)
        dots_row[me_r] = jnp.broadcast_to(row, (8, 128))
        each_partner(n_row, me_r, lambda j: d1_copy(j, me_r).start())
        each_partner(n_row, me_r, lambda j: d1_copy(j, j).wait_recv())
        dots_col[me_c] = sum(dots_row[i] for i in range(n_row))
        each_partner(n_col, me_c, lambda j: d2_copy(j, me_c).start())
        each_partner(n_col, me_c, lambda j: d2_copy(j, j).wait_recv())
        sums = jnp.broadcast_to(sum(dots_col[i] for i in range(n_col))[0:1], (tasks, 128))
        pq, rq, qq, rr = (
            jnp.sum(jnp.where(lane == task + tasks * i, sums, 0.0), axis=1, keepdims=True)
            for i in range(4))
        size = rr / pq
        new = jnp.maximum(rr - 2.0 * size * rq + size * size * qq, 0.0)
        ratio = new / rr
        for t in range(own_tiles):
            part = slice(128 * t, 128 * (t + 1))
            p = dir_ref[:, part]
            r = res[:, part] - size * images[t]
            sol[:, part] = sol[:, part] + size * p
            res[:, part] = r
            dir_ref[:, part] = r + ratio * p

        each_partner(n_row, me_r, lambda j: gather_row(j, me_r).wait_send())
        each_partner(n_col, me_c, lambda j: gather_col(j, me_c).wait_send())
        each_partner(n_col, me_c, lambda j: f_send(j, me_c).wait_send())
        each_partner(n_row, me_r, lambda j: b_send(j, me_r).wait_send())
        each_partner(n_row, me_r, lambda j: d1_copy(j, me_r).wait_send())
        each_partner(n_col, me_c, lambda j: d2_copy(j, me_c).wait_send())

        @pl.when(step + 1 < ITERS)
        def _():
            start_gather()
        return carry

    lax.fori_loop(0, ITERS, one_step, 0)


def slot_table(own, other, live, per_tile, shift, empty):
    slot = jnp.arange(own.shape[0], dtype=jnp.int32)
    same = (own[:, None] == own[None, :]) & (slot[None, :] < slot[:, None])
    key = own * per_tile + jnp.sum(same.astype(jnp.int32), axis=1)
    code = (slot << shift) + jnp.where(live, other, empty)
    return jnp.sum(jnp.where(key[None, :] == slot[:, None], code[None, :], 0), axis=1)


def per_device(n_row, n_col, scores, tile_values, tile_rows, tile_cols, tile_count):
    tiles = tile_values[0, 0]
    rows, cols = tile_rows[0, 0], tile_cols[0, 0]
    slots = tiles.shape[0]
    tasks, piece = scores.shape
    own_tiles = piece // 128
    row_tiles, col_tiles = own_tiles * n_col, own_tiles * n_row
    per_col = slots // col_tiles
    live = jnp.arange(slots, dtype=jnp.int32) < tile_count[0, 0]
    row_table = slot_table(rows, cols, live, PER_ROW, 6, col_tiles)
    col_table = slot_table(cols, rows, live, per_col, 7, row_tiles)
    f32 = jnp.float32
    dma = pltpu.SemaphoreType.DMA
    vmem = pl.BlockSpec(memory_space=pltpu.VMEM)
    smem = pl.BlockSpec(memory_space=pltpu.SMEM)
    return pl.pallas_call(
        functools.partial(cg_kernel, n_row, n_col, per_col),
        out_shape=(
            jax.ShapeDtypeStruct((tasks, piece), f32),
            jax.ShapeDtypeStruct((tasks, piece), f32),
        ),
        in_specs=[smem, smem, vmem, pl.BlockSpec(memory_space=pl.ANY)],
        out_specs=(vmem, vmem),
        scratch_shapes=[
            pltpu.VMEM((slots, 128, 128), jnp.bfloat16),
            pltpu.VMEM((col_tiles + 1, tasks, 128), jnp.bfloat16),
            pltpu.VMEM((row_tiles + 1, tasks, 128), jnp.bfloat16),
            pltpu.VMEM((row_tiles, tasks, 128), SUM_TYPE),
            pltpu.VMEM((col_tiles, tasks, 128), SUM_TYPE),
            pltpu.VMEM((n_col, own_tiles, tasks, 128), SUM_TYPE),
            pltpu.VMEM((n_row, own_tiles, tasks, 128), SUM_TYPE),
            pltpu.VMEM((n_col, 8, 128), f32),
            pltpu.VMEM((n_row, 8, 128), f32),
            pltpu.VMEM((n_col, 8, 128), f32),
            pltpu.VMEM((n_row, 8, 128), f32),
            pltpu.VMEM((2, 16, 128), jnp.bfloat16),
            pltpu.VMEM((tasks, piece), f32),
            pltpu.VMEM((8, 128), f32),
            pltpu.VMEM((n_row, 8, 128), f32),
            pltpu.VMEM((n_col, 8, 128), f32),
            dma((8,)),
            dma((n_row,)), dma((n_row,)), dma((n_col,)), dma((n_col,)),
            dma((n_col,)), dma((n_col,)), dma((n_row,)), dma((n_row,)),
            dma((n_col,)), dma((n_col,)), dma((n_row,)), dma((n_row,)),
            dma((n_row,)), dma((n_row,)), dma((n_col,)), dma((n_col,)),
        ],
        compiler_params=pltpu.CompilerParams(
            collective_id=0, has_side_effects=True, vmem_limit_bytes=56 * 1024 * 1024
        ),
    )(row_table, col_table, scores, tiles)


def solution(mesh):
    return jax.shard_map(
        functools.partial(per_device, mesh.shape["row"], mesh.shape["col"]),
        mesh=mesh,
        in_specs=(
            P(None, ("row", "col")),
            P("row", "col", None, None, None),
            P("row", "col", None),
            P("row", "col", None),
            P("row", "col"),
        ),
        out_specs=(P(None, ("row", "col")), P(None, ("row", "col"))),
        check_vma=False,
    )
```

```python
import functools

import jax
import jax.numpy as jnp
from jax import lax
from jax.experimental import pallas as pl
from jax.experimental.pallas import tpu as pltpu
from jax.sharding import PartitionSpec as P

PER_ROW = 5
ITERS = 3
MESH = pl.DeviceIdType.MESH
F_TYPE = jnp.bfloat16
B_TYPE = jnp.float32

coupling = 0.2


def spread(n):
    fast = 2 if n <= 8 else 4
    return n // fast, fast


def partner(me, k, n):
    slow, fast = spread(n)
    bits = fast.bit_length() - 1
    a = ((me >> bits) + slow // 2 + (k >> bits)) & (slow - 1)
    b = (me + fast // 2 + k) & (fast - 1)
    return a * fast + b


def own_turn(n):
    slow, fast = spread(n)
    return (slow - slow // 2) % slow * fast + (fast - fast // 2) % fast


def slot_table(own, other, live, per_tile, shift, empty):
    n = own.shape[1]
    here = lax.broadcasted_iota(jnp.int32, (n, n), 0)
    there = lax.broadcasted_iota(jnp.int32, (n, n), 1)

    def down(line):
        return jnp.sum(jnp.where(here == there, line, 0), axis=1, keepdims=True)

    own_down, other_down = down(own), down(other)
    earlier = (own_down == own) & (there < here)
    key = own_down * per_tile + jnp.sum(jnp.where(earlier, 1, 0), axis=1, keepdims=True)
    slot = here[:, :1]
    code = (slot << shift) + jnp.where(slot < live, other_down, empty)
    return jnp.sum(jnp.where(key == there, code, 0), axis=0, keepdims=True)


def copy_kernel(sol_in, res_in, sol, res):
    sol[...] = sol_in[...]
    res[...] = res_in[...]


def cg_kernel(
    n_row, n_col, per_col,
    count, rows, cols, scores, tiles_hbm, sol, res,
    tiles, x_col, x_row, f_part, b_part, f_recv, b_recv,
    df_part, db_part, df_recv, db_recv, ones, dir_ref, degree, dots_row, dots_col,
    row_codes, col_codes, row_table, col_table,
    tile_sem, table_sem,
    agr_send, agr_recv, agc_send, agc_recv,
    rsf_send, rsf_recv, rsb_send, rsb_recv,
    dgf_send, dgf_recv, dgb_send, dgb_recv,
    d1_send, d1_recv, d2_send, d2_recv,
):
    me_r = lax.axis_index("row")
    me_c = lax.axis_index("col")
    tasks = scores.shape[0]
    own_tiles = scores.shape[1] // 128
    slots = tiles.shape[0]
    col_tiles = b_part.shape[0]
    row_tiles = f_part.shape[0]
    chunk = slots // tile_sem.shape[0]

    def tile_copy(i):
        part = pl.ds(i * chunk, chunk)
        return pltpu.make_async_copy(tiles_hbm.at[part], tiles.at[part], tile_sem.at[i])

    for i in range(tile_sem.shape[0]):
        tile_copy(i).start()

    barrier = pltpu.get_barrier_semaphore()

    def greet(axis, n, own):
        def one(k, carry):
            @pl.when(k != own_turn(n))
            def _():
                j = partner(own, k, n)
                target = (me_r, j) if axis == "col" else (j, me_c)
                pl.semaphore_signal(barrier, inc=1, device_id=target, device_id_type=MESH)
            return carry

        lax.fori_loop(0, n, one, 0)

    greet("col", n_col, me_c)
    greet("row", n_row, me_r)

    x_col[col_tiles] = jnp.zeros((tasks, 128), jnp.bfloat16)
    x_row[row_tiles] = jnp.zeros((tasks, 128), jnp.bfloat16)
    live = count[0, 0]
    row_codes[...] = slot_table(rows[...], cols[...], live, PER_ROW, 6, col_tiles)
    col_codes[...] = slot_table(cols[...], rows[...], live, per_col, 7, row_tiles)
    table_copies = (
        pltpu.make_async_copy(row_codes, row_table, table_sem.at[0]),
        pltpu.make_async_copy(col_codes, col_table, table_sem.at[1]),
    )
    for copy in table_copies:
        copy.start()
    ones[0] = jnp.ones((16, 128), jnp.bfloat16)
    ones[1] = jnp.zeros((16, 128), jnp.bfloat16)
    dir_ref[...] = scores[...]
    res[...] = scores[...]
    sol[...] = jnp.zeros_like(sol)

    pl.semaphore_wait(barrier, n_row + n_col - 2)

    def each_partner(n, own, action):
        def one(k, carry):
            @pl.when(k != own_turn(n))
            def _():
                action(partner(own, k, n))
            return carry

        lax.fori_loop(0, n, one, 0)

    own_col = pl.ds(me_r * own_tiles, own_tiles)
    own_row = pl.ds(me_c * own_tiles, own_tiles)

    def gather_row(j, source):
        part = pl.ds(source * own_tiles, own_tiles)
        return pltpu.make_async_remote_copy(
            src_ref=x_col.at[part], dst_ref=x_col.at[part],
            send_sem=agr_send.at[j], recv_sem=agr_recv.at[source],
            device_id=(j, me_c), device_id_type=MESH,
        )

    def gather_col(j, source):
        part = pl.ds(source * own_tiles, own_tiles)
        return pltpu.make_async_remote_copy(
            src_ref=x_row.at[part], dst_ref=x_row.at[part],
            send_sem=agc_send.at[j], recv_sem=agc_recv.at[source],
            device_id=(me_r, j), device_id_type=MESH,
        )

    def send_pieces(j, source, part, recv, send_sem, recv_sem, axis):
        return pltpu.make_async_remote_copy(
            src_ref=part, dst_ref=recv.at[source],
            send_sem=send_sem.at[j], recv_sem=recv_sem.at[source],
            device_id=(me_r, j) if axis == "col" else (j, me_c), device_id_type=MESH,
        )

    def f_send(j, source):
        return send_pieces(
            j, source, f_part.at[pl.ds(j * own_tiles, own_tiles)], f_recv, rsf_send, rsf_recv, "col")

    def b_send(j, source):
        return send_pieces(
            j, source, b_part.at[pl.ds(j * own_tiles, own_tiles)], b_recv, rsb_send, rsb_recv, "row")

    def df_send(j, source):
        return send_pieces(j, source, df_part.at[j], df_recv, dgf_send, dgf_recv, "col")

    def db_send(j, source):
        return send_pieces(j, source, db_part.at[j], db_recv, dgb_send, dgb_recv, "row")

    def d1_copy(j, source):
        return send_pieces(j, source, dots_row.at[me_r], dots_row, d1_send, d1_recv, "row")

    def d2_copy(j, source):
        return send_pieces(j, source, dots_col.at[me_c], dots_col, d2_send, d2_recv, "col")

    def start_gather():
        for t in range(own_tiles):
            piece = dir_ref[:, 128 * t : 128 * (t + 1)].astype(jnp.bfloat16)
            x_col[me_r * own_tiles + t] = piece
            x_row[me_c * own_tiles + t] = piece
        each_partner(n_row, me_r, lambda j: gather_row(j, me_r).start())
        each_partner(n_col, me_c, lambda j: gather_col(j, me_c).start())

    def forward_tile(row, weigh):
        fields, weights = [], []
        for i in range(PER_ROW):
            code = row_table[0, row * PER_ROW + i]
            fields.append(weigh(x_col, code & 63, col_tiles))
            weights.append(tiles[code >> 6])
        return lax.dot_general(
            jnp.concatenate(fields, axis=1), jnp.concatenate(weights, axis=1),
            (((1,), (1,)), ((), ())), preferred_element_type=jnp.float32)

    def backward_tile(col, weigh):
        fields, weights = [], []
        for i in range(per_col):
            code = col_table[0, col * per_col + i]
            fields.append(weigh(x_row, code & 127, row_tiles))
            weights.append(tiles[code >> 7])
        return jnp.dot(
            jnp.concatenate(fields, axis=1), jnp.concatenate(weights, axis=0),
            preferred_element_type=jnp.float32)

    def field_of(x_ref, index, limit):
        return x_ref[index]

    def field_and_ones(x_ref, index, limit):
        unit = ones[jnp.where(index == limit, 1, 0)]
        return jnp.concatenate([x_ref[index], unit], axis=0)

    start_gather()
    for i in range(tile_sem.shape[0]):
        tile_copy(i).wait()

    for copy in table_copies:
        copy.wait()

    def product_group(n, own, tile_of, part, send, first, d_part, d_send):
        def one(k, carry):
            j = partner(own, k, n)
            for t in range(own_tiles):
                product = tile_of(j * own_tiles + t, field_and_ones if first else field_of)
                part[j * own_tiles + t] = product[:tasks].astype(part.dtype)
                if first:
                    d_part[j, t : t + 1, :] = product[tasks : tasks + 1]
            if first:
                d_part[j, own_tiles:, :] = jnp.zeros((8 - own_tiles, 128), jnp.float32)

            @pl.when(k != own_turn(n))
            def _():
                send(j, own).start()
                if first:
                    d_send(j, own).start()
            return carry

        lax.fori_loop(0, n, one, 0)

    def gather_sums(n, own, send, recv, totals):
        def one(k, sums):
            j = (own + 1 + k) & (n - 1)
            send(j, j).wait_recv()
            return tuple(s + recv[j, t].astype(jnp.float32) for t, s in enumerate(sums))

        return lax.fori_loop(0, n - 1, one, totals)

    lane = lax.broadcasted_iota(jnp.int32, (tasks, 128), 1)
    task = lax.broadcasted_iota(jnp.int32, (tasks, 128), 0)

    def one_step(step, first):
        each_partner(n_row, me_r, lambda j: gather_row(j, j).wait_recv())
        product_group(n_col, me_c, forward_tile, f_part, f_send, first, df_part, df_send)
        each_partner(n_col, me_c, lambda j: gather_col(j, j).wait_recv())
        product_group(n_row, me_r, backward_tile, b_part, b_send, first, db_part, db_send)

        if first:
            total = df_part[me_c] + db_part[me_r]

            def add_f(k, t):
                j = (me_c + 1 + k) & (n_col - 1)
                df_send(j, j).wait_recv()
                return t + df_recv[j]

            def add_b(k, t):
                j = (me_r + 1 + k) & (n_row - 1)
                db_send(j, j).wait_recv()
                return t + db_recv[j]

            total = lax.fori_loop(0, n_row - 1, add_b, total)
            total = lax.fori_loop(0, n_col - 1, add_f, total)
            degree[...] = 0.5 * total

        totals = tuple(
            f_part[me_c * own_tiles + t].astype(jnp.float32)
            + b_part[me_r * own_tiles + t].astype(jnp.float32)
            for t in range(own_tiles))
        totals = gather_sums(n_row, me_r, b_send, b_recv, totals)
        totals = gather_sums(n_col, me_c, f_send, f_recv, totals)

        pq = jnp.zeros((tasks, 128), jnp.float32)
        rq, qq, rr = pq, pq, pq
        images = []
        for t in range(own_tiles):
            part = slice(128 * t, 128 * (t + 1))
            p, r = dir_ref[:, part], res[:, part]
            q = p + coupling * (degree[t : t + 1, :] * p - 0.5 * totals[t])
            images.append(q)
            pq, rq, qq, rr = pq + p * q, rq + r * q, qq + q * q, rr + r * r
        row = jnp.zeros((tasks, 128), jnp.float32)
        for i, s in enumerate((pq, rq, qq, rr)):
            row = jnp.where(lane == task + tasks * i, jnp.sum(s, axis=1, keepdims=True), row)
        row = jnp.sum(row, axis=0, keepdims=True)
        dots_row[me_r] = jnp.broadcast_to(row, (8, 128))
        each_partner(n_row, me_r, lambda j: d1_copy(j, me_r).start())
        each_partner(n_row, me_r, lambda j: d1_copy(j, j).wait_recv())
        dots_col[me_c] = sum(dots_row[i] for i in range(n_row))
        each_partner(n_col, me_c, lambda j: d2_copy(j, me_c).start())
        each_partner(n_col, me_c, lambda j: d2_copy(j, j).wait_recv())
        sums = jnp.broadcast_to(sum(dots_col[i] for i in range(n_col))[0:1], (tasks, 128))
        pq, rq, qq, rr = (
            jnp.sum(jnp.where(lane == task + tasks * i, sums, 0.0), axis=1, keepdims=True)
            for i in range(4))
        size = rr / pq
        new = jnp.maximum(rr - 2.0 * size * rq + size * size * qq, 0.0)
        ratio = new / rr
        for t in range(own_tiles):
            part = slice(128 * t, 128 * (t + 1))
            p = dir_ref[:, part]
            r = res[:, part] - size * images[t]
            sol[:, part] = sol[:, part] + size * p
            res[:, part] = r
            dir_ref[:, part] = r + ratio * p

        each_partner(n_row, me_r, lambda j: gather_row(j, me_r).wait_send())
        each_partner(n_col, me_c, lambda j: gather_col(j, me_c).wait_send())
        each_partner(n_col, me_c, lambda j: f_send(j, me_c).wait_send())
        each_partner(n_row, me_r, lambda j: b_send(j, me_r).wait_send())
        each_partner(n_row, me_r, lambda j: d1_copy(j, me_r).wait_send())
        each_partner(n_col, me_c, lambda j: d2_copy(j, me_c).wait_send())

        if first:
            each_partner(n_col, me_c, lambda j: df_send(j, me_c).wait_send())
            each_partner(n_row, me_r, lambda j: db_send(j, me_r).wait_send())

        @pl.when(step + 1 < ITERS)
        def _():
            start_gather()

    one_step(0, True)

    def later_step(step, carry):
        one_step(step, False)
        return carry

    lax.fori_loop(1, ITERS, later_step, 0)


def per_device(n_row, n_col, scores, tile_values, tile_rows, tile_cols, tile_count):
    tiles = tile_values[0, 0]
    rows, cols = tile_rows[0], tile_cols[0]
    slots = tiles.shape[0]
    tasks, piece = scores.shape
    own_tiles = piece // 128
    row_tiles, col_tiles = own_tiles * n_col, own_tiles * n_row
    per_col = slots // col_tiles
    f32 = jnp.float32
    dma = pltpu.SemaphoreType.DMA
    vmem = pl.BlockSpec(memory_space=pltpu.VMEM)
    smem = pl.BlockSpec(memory_space=pltpu.SMEM)
    sol, res = pl.pallas_call(
        functools.partial(cg_kernel, n_row, n_col, per_col),
        out_shape=(
            jax.ShapeDtypeStruct((tasks, piece), f32),
            jax.ShapeDtypeStruct((tasks, piece), f32),
        ),
        in_specs=[smem, vmem, vmem, vmem, pl.BlockSpec(memory_space=pl.ANY)],
        out_specs=(vmem, vmem),
        scratch_shapes=[
            pltpu.VMEM((slots, 128, 128), jnp.bfloat16),
            pltpu.VMEM((col_tiles + 1, tasks, 128), jnp.bfloat16),
            pltpu.VMEM((row_tiles + 1, tasks, 128), jnp.bfloat16),
            pltpu.VMEM((row_tiles, tasks, 128), F_TYPE),
            pltpu.VMEM((col_tiles, tasks, 128), B_TYPE),
            pltpu.VMEM((n_col, own_tiles, tasks, 128), F_TYPE),
            pltpu.VMEM((n_row, own_tiles, tasks, 128), B_TYPE),
            pltpu.VMEM((n_col, 8, 128), f32),
            pltpu.VMEM((n_row, 8, 128), f32),
            pltpu.VMEM((n_col, 8, 128), f32),
            pltpu.VMEM((n_row, 8, 128), f32),
            pltpu.VMEM((2, 16, 128), jnp.bfloat16),
            pltpu.VMEM((tasks, piece), f32),
            pltpu.VMEM((8, 128), f32),
            pltpu.VMEM((n_row, 8, 128), f32),
            pltpu.VMEM((n_col, 8, 128), f32),
            pltpu.VMEM((1, slots), jnp.int32),
            pltpu.VMEM((1, slots), jnp.int32),
            pltpu.SMEM((1, slots), jnp.int32),
            pltpu.SMEM((1, slots), jnp.int32),
            dma((8,)), dma((2,)),
            dma((n_row,)), dma((n_row,)), dma((n_col,)), dma((n_col,)),
            dma((n_col,)), dma((n_col,)), dma((n_row,)), dma((n_row,)),
            dma((n_col,)), dma((n_col,)), dma((n_row,)), dma((n_row,)),
            dma((n_row,)), dma((n_row,)), dma((n_col,)), dma((n_col,)),
        ],
        compiler_params=pltpu.CompilerParams(
            collective_id=0, has_side_effects=True, vmem_limit_bytes=56 * 1024 * 1024
        ),
    )(tile_count, rows, cols, scores, tiles)
    return pl.pallas_call(
        copy_kernel,
        out_shape=(
            jax.ShapeDtypeStruct((tasks, piece), f32),
            jax.ShapeDtypeStruct((tasks, piece), f32),
        ),
        in_specs=[vmem, vmem],
        out_specs=(vmem, vmem),
    )(sol, res)


def solution(mesh):
    return jax.shard_map(
        functools.partial(per_device, mesh.shape["row"], mesh.shape["col"]),
        mesh=mesh,
        in_specs=(
            P(None, ("row", "col")),
            P("row", "col", None, None, None),
            P("row", "col", None),
            P("row", "col", None),
            P("row", "col"),
        ),
        out_specs=(P(None, ("row", "col")), P(None, ("row", "col"))),
        check_vma=False,
    )
```

```python
import functools

import jax
import jax.numpy as jnp
from jax import lax
from jax.experimental import pallas as pl
from jax.experimental.pallas import tpu as pltpu
from jax.sharding import PartitionSpec as P

PER_ROW = 5
ITERS = 3
MESH = pl.DeviceIdType.MESH
F_TYPE = jnp.bfloat16
B_TYPE = jnp.float32

coupling = 0.2


def spread(n):
    fast = 2 if n <= 8 else 4
    return n // fast, fast


def partner(me, k, n):
    slow, fast = spread(n)
    bits = fast.bit_length() - 1
    a = ((me >> bits) + slow // 2 + (k >> bits)) & (slow - 1)
    b = (me + fast // 2 + k) & (fast - 1)
    return a * fast + b


def own_turn(n):
    slow, fast = spread(n)
    return (slow - slow // 2) % slow * fast + (fast - fast // 2) % fast


def slot_table(own, other, live, per_tile, shift, empty):
    n = own.shape[1]
    here = lax.broadcasted_iota(jnp.int32, (n, n), 0)
    there = lax.broadcasted_iota(jnp.int32, (n, n), 1)

    def down(line):
        return jnp.sum(jnp.where(here == there, line, 0), axis=1, keepdims=True)

    own_down, other_down = down(own), down(other)
    earlier = (own_down == own) & (there < here)
    key = own_down * per_tile + jnp.sum(jnp.where(earlier, 1, 0), axis=1, keepdims=True)
    slot = here[:, :1]
    code = (slot << shift) + jnp.where(slot < live, other_down, empty)
    return jnp.sum(jnp.where(key == there, code, 0), axis=0, keepdims=True)


def copy_kernel(sol_in, res_in, sol, res):
    sol[...] = sol_in[...]
    res[...] = res_in[...]


def pick(index, values):
    value = values[-1]
    for i, v in enumerate(values[:-1]):
        value = jnp.where(index == i, v, value)
    return value


def cg_kernel(
    n_row, n_col, per_col,
    count, rows, cols, scores, tiles_hbm, sol, res,
    tiles, x_col, x_row, f_part, b_part, f_recv, b_recv, pair,
    df_part, db_part, df_recv, db_recv, ones, dir_ref, degree, dots_row, dots_col,
    row_codes, col_codes, row_table, col_table,
    tile_sem, table_sem,
    agr_send, agr_recv, agc_send, agc_recv,
    rsf_send, rsf_recv, rsb_send, rsb_recv, pair_send, pair_recv,
    dgf_send, dgf_recv, dgb_send, dgb_recv,
    d1_send, d1_recv, d2_send, d2_recv,
):
    me_r = lax.axis_index("row")
    me_c = lax.axis_index("col")
    y, core = me_r >> 1, me_r & 1
    chips = n_row // 2
    sibling = me_r + 1 - 2 * core
    far_first = sorted(range(1, chips), key=lambda d: -min(d, chips - d))
    tasks = scores.shape[0]
    own_tiles = scores.shape[1] // 128
    slots = tiles.shape[0]
    col_tiles = b_part.shape[0]
    row_tiles = f_part.shape[0]
    chunk = slots // tile_sem.shape[0]

    def tile_copy(i):
        part = pl.ds(i * chunk, chunk)
        return pltpu.make_async_copy(tiles_hbm.at[part], tiles.at[part], tile_sem.at[i])

    for i in range(tile_sem.shape[0]):
        tile_copy(i).start()

    barrier = pltpu.get_barrier_semaphore()

    def greet(axis, n, own):
        def one(k, carry):
            @pl.when(k != own_turn(n))
            def _():
                j = partner(own, k, n)
                target = (me_r, j) if axis == "col" else (j, me_c)
                pl.semaphore_signal(barrier, inc=1, device_id=target, device_id_type=MESH)
            return carry

        lax.fori_loop(0, n, one, 0)

    greet("col", n_col, me_c)
    greet("row", n_row, me_r)

    x_col[col_tiles] = jnp.zeros((tasks, 128), jnp.bfloat16)
    x_row[row_tiles] = jnp.zeros((tasks, 128), jnp.bfloat16)
    live = count[0, 0]
    row_codes[...] = slot_table(rows[...], cols[...], live, PER_ROW, 6, col_tiles)
    col_codes[...] = slot_table(cols[...], rows[...], live, per_col, 7, row_tiles)
    table_copies = (
        pltpu.make_async_copy(row_codes, row_table, table_sem.at[0]),
        pltpu.make_async_copy(col_codes, col_table, table_sem.at[1]),
    )
    for copy in table_copies:
        copy.start()
    ones[0] = jnp.ones((16, 128), jnp.bfloat16)
    ones[1] = jnp.zeros((16, 128), jnp.bfloat16)
    dir_ref[...] = scores[...]
    res[...] = scores[...]
    sol[...] = jnp.zeros_like(sol)

    pl.semaphore_wait(barrier, n_row + n_col - 2)

    def each_partner(n, own, action):
        def one(k, carry):
            @pl.when(k != own_turn(n))
            def _():
                action(partner(own, k, n))
            return carry

        lax.fori_loop(0, n, one, 0)

    own_col = pl.ds(me_r * own_tiles, own_tiles)
    own_row = pl.ds(me_c * own_tiles, own_tiles)

    def gather_row(j, source, sem):
        part = pl.ds(source * own_tiles, own_tiles)
        return pltpu.make_async_remote_copy(
            src_ref=x_col.at[part], dst_ref=x_col.at[part],
            send_sem=agr_send.at[sem], recv_sem=agr_recv.at[source],
            device_id=(j, me_c), device_id_type=MESH,
        )

    def at_chip(d, on_core):
        return ((y + d) & (chips - 1)) * 2 + on_core

    def gather_col(j, source):
        part = pl.ds(source * own_tiles, own_tiles)
        return pltpu.make_async_remote_copy(
            src_ref=x_row.at[part], dst_ref=x_row.at[part],
            send_sem=agc_send.at[j], recv_sem=agc_recv.at[source],
            device_id=(me_r, j), device_id_type=MESH,
        )

    def send_pieces(j, source, part, recv, send_sem, recv_sem, axis):
        return pltpu.make_async_remote_copy(
            src_ref=part, dst_ref=recv.at[source],
            send_sem=send_sem.at[j], recv_sem=recv_sem.at[source],
            device_id=(me_r, j) if axis == "col" else (j, me_c), device_id_type=MESH,
        )

    def f_send(j, source):
        return send_pieces(
            j, source, f_part.at[pl.ds(j * own_tiles, own_tiles)], f_recv, rsf_send, rsf_recv, "col")

    def b_send(d):
        j = at_chip(d, core)
        return pltpu.make_async_remote_copy(
            src_ref=b_part.at[pl.ds(j * own_tiles, own_tiles)], dst_ref=b_recv.at[y],
            send_sem=rsb_send.at[d], recv_sem=rsb_recv.at[y],
            device_id=(j, me_c), device_id_type=MESH,
        )

    def b_arrival(d):
        source = (y + d) & (chips - 1)
        return pltpu.make_async_remote_copy(
            src_ref=b_part.at[pl.ds(me_r * own_tiles, own_tiles)], dst_ref=b_recv.at[source],
            send_sem=rsb_send.at[d], recv_sem=rsb_recv.at[source],
            device_id=(at_chip(d, core), me_c), device_id_type=MESH,
        )

    def pair_copy(d):
        j = at_chip(d, 1 - core)
        return pltpu.make_async_remote_copy(
            src_ref=b_part.at[pl.ds(j * own_tiles, own_tiles)], dst_ref=pair.at[d],
            send_sem=pair_send.at[d], recv_sem=pair_recv.at[d],
            device_id=(sibling, me_c), device_id_type=MESH,
        )

    def df_send(j, source):
        return send_pieces(j, source, df_part.at[j], df_recv, dgf_send, dgf_recv, "col")

    def db_send(j, source):
        return send_pieces(j, source, db_part.at[j], db_recv, dgb_send, dgb_recv, "row")

    def d1_copy(j, source):
        return send_pieces(j, source, dots_row.at[me_r], dots_row, d1_send, d1_recv, "row")

    def d2_copy(j, source):
        return send_pieces(j, source, dots_col.at[me_c], dots_col, d2_send, d2_recv, "col")

    def start_gather():
        for t in range(own_tiles):
            piece = dir_ref[:, 128 * t : 128 * (t + 1)].astype(jnp.bfloat16)
            x_col[me_r * own_tiles + t] = piece
            x_row[me_c * own_tiles + t] = piece
        for d in far_first:
            gather_row(at_chip(d, core), me_r, at_chip(d, core)).start()
        gather_row(sibling, me_r, sibling).start()
        each_partner(n_col, me_c, lambda j: gather_col(j, me_c).start())

    def pass_row_on():
        for d in reversed(far_first):
            source = at_chip(d, core)
            gather_row(source, source, source).wait_recv()
            gather_row(sibling, source, at_chip(d, 1 - core)).start()
        gather_row(sibling, sibling, sibling).wait_recv()
        for d in reversed(far_first):
            source = at_chip(d, 1 - core)
            gather_row(sibling, source, source).wait_recv()

    def end_gather_sends():
        for d in far_first:
            gather_row(at_chip(d, core), me_r, at_chip(d, core)).wait_send()
            gather_row(sibling, at_chip(d, core), at_chip(d, 1 - core)).wait_send()
        gather_row(sibling, me_r, sibling).wait_send()
        each_partner(n_col, me_c, lambda j: gather_col(j, me_c).wait_send())

    def forward_tile(row, weigh):
        fields, weights = [], []
        for i in range(PER_ROW):
            code = row_table[0, row * PER_ROW + i]
            fields.append(weigh(x_col, code & 63, col_tiles))
            weights.append(tiles[code >> 6])
        return lax.dot_general(
            jnp.concatenate(fields, axis=1), jnp.concatenate(weights, axis=1),
            (((1,), (1,)), ((), ())), preferred_element_type=jnp.float32)

    def backward_tile(col, weigh):
        fields, weights = [], []
        for i in range(per_col):
            code = col_table[0, col * per_col + i]
            fields.append(weigh(x_row, code & 127, row_tiles))
            weights.append(tiles[code >> 7])
        return jnp.dot(
            jnp.concatenate(fields, axis=1), jnp.concatenate(weights, axis=0),
            preferred_element_type=jnp.float32)

    def field_of(x_ref, index, limit):
        return x_ref[index]

    def field_and_ones(x_ref, index, limit):
        unit = ones[jnp.where(index == limit, 1, 0)]
        return jnp.concatenate([x_ref[index], unit], axis=0)

    start_gather()
    for i in range(tile_sem.shape[0]):
        tile_copy(i).wait()

    for copy in table_copies:
        copy.wait()

    def chunk_products(j, tile_of, part, first, d_part):
        for t in range(own_tiles):
            product = tile_of(j * own_tiles + t, field_and_ones if first else field_of)
            part[j * own_tiles + t] = product[:tasks].astype(part.dtype)
            if first:
                d_part[j, t : t + 1, :] = product[tasks : tasks + 1]
        if first:
            d_part[j, own_tiles:, :] = jnp.zeros((8 - own_tiles, 128), jnp.float32)

    def forward_products(first):
        def one(k, carry):
            j = partner(me_c, k, n_col)
            chunk_products(j, forward_tile, f_part, first, df_part)

            @pl.when(k != own_turn(n_col))
            def _():
                f_send(j, me_c).start()
                if first:
                    df_send(j, me_c).start()
            return carry

        lax.fori_loop(0, n_col, one, 0)

    turns = far_first + [0]
    ahead = [(d, 0) for d in turns]
    behind = [(d, 1) for d in turns]
    order = [ahead[0]]
    for i in range(1, chips):
        order += [ahead[i], behind[i - 1]]
    order.append(behind[-1])

    def backward_products(first):
        def one(k, carry):
            d = pick(k, [d for d, final in order])
            final = pick(k, [final for d, final in order])
            j = at_chip(d, core + (1 - final) * (1 - 2 * core))
            chunk_products(j, backward_tile, b_part, first, db_part)

            @pl.when(final == 0)
            def _():
                pair_copy(d).start()

            @pl.when(final == 1)
            def _():
                pair_copy(d).wait_recv()
                for t in range(own_tiles):
                    b_part[j * own_tiles + t] = b_part[j * own_tiles + t] + pair[d, t]

                @pl.when(d != 0)
                def _():
                    b_send(d).start()

            if first:

                @pl.when(j != me_r)
                def _():
                    db_send(j, me_r).start()
            return carry

        lax.fori_loop(0, n_row, one, 0)

    def gather_sums(n, own, send, recv, totals):
        def one(k, sums):
            j = (own + 1 + k) & (n - 1)
            send(j, j).wait_recv()
            return tuple(s + recv[j, t].astype(jnp.float32) for t, s in enumerate(sums))

        return lax.fori_loop(0, n - 1, one, totals)

    lane = lax.broadcasted_iota(jnp.int32, (tasks, 128), 1)
    task = lax.broadcasted_iota(jnp.int32, (tasks, 128), 0)

    def one_step(step, first):
        pass_row_on()
        forward_products(first)
        each_partner(n_col, me_c, lambda j: gather_col(j, j).wait_recv())
        backward_products(first)
        end_gather_sends()

        if first:
            total = df_part[me_c] + db_part[me_r]

            def add_f(k, t):
                j = (me_c + 1 + k) & (n_col - 1)
                df_send(j, j).wait_recv()
                return t + df_recv[j]

            def add_b(k, t):
                j = (me_r + 1 + k) & (n_row - 1)
                db_send(j, j).wait_recv()
                return t + db_recv[j]

            total = lax.fori_loop(0, n_row - 1, add_b, total)
            total = lax.fori_loop(0, n_col - 1, add_f, total)
            degree[...] = 0.5 * total

        totals = tuple(
            f_part[me_c * own_tiles + t].astype(jnp.float32)
            + b_part[me_r * own_tiles + t].astype(jnp.float32)
            for t in range(own_tiles))
        totals = gather_sums(n_col, me_c, f_send, f_recv, totals)
        for d in reversed(far_first):
            b_arrival(d).wait_recv()
            source = (y + d) & (chips - 1)
            totals = tuple(s + b_recv[source, t] for t, s in enumerate(totals))

        pq = jnp.zeros((tasks, 128), jnp.float32)
        rq, qq, rr = pq, pq, pq
        images = []
        for t in range(own_tiles):
            part = slice(128 * t, 128 * (t + 1))
            p, r = dir_ref[:, part], res[:, part]
            q = p + coupling * (degree[t : t + 1, :] * p - 0.5 * totals[t])
            images.append(q)
            pq, rq, qq, rr = pq + p * q, rq + r * q, qq + q * q, rr + r * r
        row = jnp.zeros((tasks, 128), jnp.float32)
        for i, s in enumerate((pq, rq, qq, rr)):
            row = jnp.where(lane == task + tasks * i, jnp.sum(s, axis=1, keepdims=True), row)
        row = jnp.sum(row, axis=0, keepdims=True)
        dots_row[me_r] = row
        each_partner(n_row, me_r, lambda j: d1_copy(j, me_r).start())
        each_partner(n_row, me_r, lambda j: d1_copy(j, j).wait_recv())
        dots_col[me_c] = sum(dots_row[i] for i in range(n_row))
        each_partner(n_col, me_c, lambda j: d2_copy(j, me_c).start())
        each_partner(n_col, me_c, lambda j: d2_copy(j, j).wait_recv())
        sums = jnp.broadcast_to(sum(dots_col[i] for i in range(n_col)), (tasks, 128))
        pq, rq, qq, rr = (
            jnp.sum(jnp.where(lane == task + tasks * i, sums, 0.0), axis=1, keepdims=True)
            for i in range(4))
        size = rr / pq
        new = jnp.maximum(rr - 2.0 * size * rq + size * size * qq, 0.0)
        ratio = new / rr
        moves = []
        for t in range(own_tiles):
            part = slice(128 * t, 128 * (t + 1))
            p = dir_ref[:, part]
            r = res[:, part] - size * images[t]
            moves.append(size * p)
            res[:, part] = r
            dir_ref[:, part] = r + ratio * p

        @pl.when(step + 1 < ITERS)
        def _():
            start_gather()

        for t in range(own_tiles):
            part = slice(128 * t, 128 * (t + 1))
            sol[:, part] = sol[:, part] + moves[t]
        each_partner(n_col, me_c, lambda j: f_send(j, me_c).wait_send())
        for d in range(chips):
            pair_copy(d).wait_send()
        for d in far_first:
            b_send(d).wait_send()
        each_partner(n_row, me_r, lambda j: d1_copy(j, me_r).wait_send())
        each_partner(n_col, me_c, lambda j: d2_copy(j, me_c).wait_send())
        if first:
            each_partner(n_col, me_c, lambda j: df_send(j, me_c).wait_send())
            each_partner(n_row, me_r, lambda j: db_send(j, me_r).wait_send())

    one_step(0, True)

    def later_step(step, carry):
        one_step(step, False)
        return carry

    lax.fori_loop(1, ITERS, later_step, 0)


def per_device(n_row, n_col, scores, tile_values, tile_rows, tile_cols, tile_count):
    tiles = tile_values[0, 0]
    rows, cols = tile_rows[0], tile_cols[0]
    slots = tiles.shape[0]
    tasks, piece = scores.shape
    own_tiles = piece // 128
    row_tiles, col_tiles = own_tiles * n_col, own_tiles * n_row
    per_col = slots // col_tiles
    f32 = jnp.float32
    dma = pltpu.SemaphoreType.DMA
    vmem = pl.BlockSpec(memory_space=pltpu.VMEM)
    smem = pl.BlockSpec(memory_space=pltpu.SMEM)
    sol, res = pl.pallas_call(
        functools.partial(cg_kernel, n_row, n_col, per_col),
        out_shape=(
            jax.ShapeDtypeStruct((tasks, piece), f32),
            jax.ShapeDtypeStruct((tasks, piece), f32),
        ),
        in_specs=[smem, vmem, vmem, vmem, pl.BlockSpec(memory_space=pl.ANY)],
        out_specs=(vmem, vmem),
        scratch_shapes=[
            pltpu.VMEM((slots, 128, 128), jnp.bfloat16),
            pltpu.VMEM((col_tiles + 1, tasks, 128), jnp.bfloat16),
            pltpu.VMEM((row_tiles + 1, tasks, 128), jnp.bfloat16),
            pltpu.VMEM((row_tiles, tasks, 128), F_TYPE),
            pltpu.VMEM((col_tiles, tasks, 128), B_TYPE),
            pltpu.VMEM((n_col, own_tiles, tasks, 128), F_TYPE),
            pltpu.VMEM((n_row // 2, own_tiles, tasks, 128), B_TYPE),
            pltpu.VMEM((n_row // 2, own_tiles, tasks, 128), B_TYPE),
            pltpu.VMEM((n_col, 8, 128), f32),
            pltpu.VMEM((n_row, 8, 128), f32),
            pltpu.VMEM((n_col, 8, 128), f32),
            pltpu.VMEM((n_row, 8, 128), f32),
            pltpu.VMEM((2, 16, 128), jnp.bfloat16),
            pltpu.VMEM((tasks, piece), f32),
            pltpu.VMEM((8, 128), f32),
            pltpu.VMEM((n_row, 1, 128), f32),
            pltpu.VMEM((n_col, 1, 128), f32),
            pltpu.VMEM((1, slots), jnp.int32),
            pltpu.VMEM((1, slots), jnp.int32),
            pltpu.SMEM((1, slots), jnp.int32),
            pltpu.SMEM((1, slots), jnp.int32),
            dma((8,)), dma((2,)),
            dma((n_row,)), dma((n_row,)), dma((n_col,)), dma((n_col,)),
            dma((n_col,)), dma((n_col,)), dma((n_row // 2,)), dma((n_row // 2,)),
            dma((n_row // 2,)), dma((n_row // 2,)),
            dma((n_col,)), dma((n_col,)), dma((n_row,)), dma((n_row,)),
            dma((n_row,)), dma((n_row,)), dma((n_col,)), dma((n_col,)),
        ],
        compiler_params=pltpu.CompilerParams(
            collective_id=0, has_side_effects=True, vmem_limit_bytes=56 * 1024 * 1024
        ),
    )(tile_count, rows, cols, scores, tiles)
    return pl.pallas_call(
        copy_kernel,
        out_shape=(
            jax.ShapeDtypeStruct((tasks, piece), f32),
            jax.ShapeDtypeStruct((tasks, piece), f32),
        ),
        in_specs=[vmem, vmem],
        out_specs=(vmem, vmem),
    )(sol, res)


def solution(mesh):
    return jax.shard_map(
        functools.partial(per_device, mesh.shape["row"], mesh.shape["col"]),
        mesh=mesh,
        in_specs=(
            P(None, ("row", "col")),
            P("row", "col", None, None, None),
            P("row", "col", None),
            P("row", "col", None),
            P("row", "col"),
        ),
        out_specs=(P(None, ("row", "col")), P(None, ("row", "col"))),
        check_vma=False,
    )
```

```python
import functools

import jax
import jax.numpy as jnp
from jax import lax
from jax.experimental import pallas as pl
from jax.experimental.pallas import tpu as pltpu
from jax.sharding import PartitionSpec as P

PER_ROW = 5
ITERS = 3
MESH = pl.DeviceIdType.MESH
F_TYPE = jnp.bfloat16
B_TYPE = jnp.float32

coupling = 0.2


def spread(n):
    fast = 2 if n <= 8 else 4
    return n // fast, fast


def partner(me, k, n):
    slow, fast = spread(n)
    bits = fast.bit_length() - 1
    a = ((me >> bits) + slow // 2 + (k >> bits)) & (slow - 1)
    b = (me + fast // 2 + k) & (fast - 1)
    return a * fast + b


def own_turn(n):
    slow, fast = spread(n)
    return (slow - slow // 2) % slow * fast + (fast - fast // 2) % fast


def slot_table(own, other, live, per_tile, shift, empty):
    n = own.shape[1]
    here = lax.broadcasted_iota(jnp.int32, (n, n), 0)
    there = lax.broadcasted_iota(jnp.int32, (n, n), 1)

    def down(line):
        return jnp.sum(jnp.where(here == there, line, 0), axis=1, keepdims=True)

    own_down, other_down = down(own), down(other)
    earlier = (own_down == own) & (there < here)
    key = own_down * per_tile + jnp.sum(jnp.where(earlier, 1, 0), axis=1, keepdims=True)
    slot = here[:, :1]
    code = (slot << shift) + jnp.where(slot < live, other_down, empty)
    return jnp.sum(jnp.where(key == there, code, 0), axis=0, keepdims=True)


def copy_kernel(sol_in, res_in, sol, res):
    sol[...] = sol_in[...]
    res[...] = res_in[...]


def pick(index, values):
    value = values[-1]
    for i, v in enumerate(values[:-1]):
        value = jnp.where(index == i, v, value)
    return value


def cg_kernel(
    n_row, n_col, per_col,
    count, rows, cols, scores, tiles_hbm, sol, res,
    tiles, x_col, x_row, f_part, b_part, f_recv, b_recv, pair,
    df_part, db_part, df_recv, db_recv, ones, dir_ref, degree, dots_row, dots_col,
    row_codes, col_codes, row_table, col_table,
    tile_sem, table_sem,
    agr_send, agr_recv, agc_send, agc_recv,
    rsf_send, rsf_recv, rsb_send, rsb_recv, pair_send, pair_recv,
    dgf_send, dgf_recv, dgb_send, dgb_recv,
    d1_send, d1_recv, d2_send, d2_recv,
):
    me_r = lax.axis_index("row")
    me_c = lax.axis_index("col")
    y, core = me_r >> 1, me_r & 1
    chips = n_row // 2
    sibling = me_r + 1 - 2 * core
    far_first = sorted(range(1, chips), key=lambda d: -min(d, chips - d))
    tasks = scores.shape[0]
    own_tiles = scores.shape[1] // 128
    slots = tiles.shape[0]
    col_tiles = b_part.shape[0]
    row_tiles = f_part.shape[0]
    chunk = slots // tile_sem.shape[0]

    def tile_copy(i):
        part = pl.ds(i * chunk, chunk)
        return pltpu.make_async_copy(tiles_hbm.at[part], tiles.at[part], tile_sem.at[i])

    for i in range(tile_sem.shape[0]):
        tile_copy(i).start()

    barrier = pltpu.get_barrier_semaphore()

    def greet(axis, n, own):
        def one(k, carry):
            @pl.when(k != own_turn(n))
            def _():
                j = partner(own, k, n)
                target = (me_r, j) if axis == "col" else (j, me_c)
                pl.semaphore_signal(barrier, inc=1, device_id=target, device_id_type=MESH)
            return carry

        lax.fori_loop(0, n, one, 0)

    greet("col", n_col, me_c)
    greet("row", n_row, me_r)

    x_col[col_tiles] = jnp.zeros((tasks, 128), jnp.bfloat16)
    x_row[row_tiles] = jnp.zeros((tasks, 128), jnp.bfloat16)
    ones[0] = jnp.ones((16, 128), jnp.bfloat16)
    ones[1] = jnp.zeros((16, 128), jnp.bfloat16)
    dir_ref[...] = scores[...]
    res[...] = scores[...]
    sol[...] = jnp.zeros_like(sol)

    pl.semaphore_wait(barrier, n_row + n_col - 2)

    def each_partner(n, own, action):
        def one(k, carry):
            @pl.when(k != own_turn(n))
            def _():
                action(partner(own, k, n))
            return carry

        lax.fori_loop(0, n, one, 0)

    own_col = pl.ds(me_r * own_tiles, own_tiles)
    own_row = pl.ds(me_c * own_tiles, own_tiles)

    def gather_row(j, source, sem):
        part = pl.ds(source * own_tiles, own_tiles)
        return pltpu.make_async_remote_copy(
            src_ref=x_col.at[part], dst_ref=x_col.at[part],
            send_sem=agr_send.at[sem], recv_sem=agr_recv.at[source],
            device_id=(j, me_c), device_id_type=MESH,
        )

    def all_of(ref, number, send_sem, recv_sem):
        part = ref.at[pl.ds(0, number)]
        return pltpu.make_async_remote_copy(
            src_ref=part, dst_ref=part, send_sem=send_sem.at[0], recv_sem=recv_sem.at[0],
            device_id=(sibling, me_c), device_id_type=MESH,
        )

    others_row, others_col = n_row - 1, n_col - 1
    all_cols = all_of(x_row, others_col * own_tiles, agc_send, agc_recv)
    all_f = all_of(f_part, others_col * own_tiles, rsf_send, rsf_send)
    all_df = all_of(df_recv, others_col, dgf_send, dgf_recv)
    all_db = all_of(db_recv, others_row, dgb_send, dgb_recv)
    all_d1 = all_of(dots_row, others_row, d1_send, d1_recv)
    all_d2 = all_of(dots_col, others_col, d2_send, d2_recv)

    def at_chip(d, on_core):
        return ((y + d) & (chips - 1)) * 2 + on_core

    def gather_col(j, source):
        part = pl.ds(source * own_tiles, own_tiles)
        return pltpu.make_async_remote_copy(
            src_ref=x_row.at[part], dst_ref=x_row.at[part],
            send_sem=agc_send.at[0], recv_sem=agc_recv.at[0],
            device_id=(me_r, j), device_id_type=MESH,
        )

    def send_pieces(j, source, part, recv, send_sem, recv_sem, axis):
        return pltpu.make_async_remote_copy(
            src_ref=part, dst_ref=recv.at[source],
            send_sem=send_sem.at[0], recv_sem=recv_sem.at[source if recv is f_recv else 0],
            device_id=(me_r, j) if axis == "col" else (j, me_c), device_id_type=MESH,
        )

    def f_send(j, source):
        return send_pieces(
            j, source, f_part.at[pl.ds(j * own_tiles, own_tiles)], f_recv, rsf_send, rsf_recv, "col")

    def b_send(d):
        j = at_chip(d, core)
        return pltpu.make_async_remote_copy(
            src_ref=b_part.at[pl.ds(j * own_tiles, own_tiles)], dst_ref=b_recv.at[y],
            send_sem=rsb_send.at[d], recv_sem=rsb_recv.at[y],
            device_id=(j, me_c), device_id_type=MESH,
        )

    def b_arrival(d):
        source = (y + d) & (chips - 1)
        return pltpu.make_async_remote_copy(
            src_ref=b_part.at[pl.ds(me_r * own_tiles, own_tiles)], dst_ref=b_recv.at[source],
            send_sem=rsb_send.at[d], recv_sem=rsb_recv.at[source],
            device_id=(at_chip(d, core), me_c), device_id_type=MESH,
        )

    def pair_copy(d):
        j = at_chip(d, 1 - core)
        return pltpu.make_async_remote_copy(
            src_ref=b_part.at[pl.ds(j * own_tiles, own_tiles)], dst_ref=pair.at[d],
            send_sem=pair_send.at[d], recv_sem=pair_recv.at[d],
            device_id=(sibling, me_c), device_id_type=MESH,
        )

    def df_send(j, source):
        return send_pieces(j, source, df_part.at[j], df_recv, dgf_send, dgf_recv, "col")

    def db_send(j, source):
        return send_pieces(j, source, db_part.at[j], db_recv, dgb_send, dgb_recv, "row")

    def d1_copy(j, source):
        return send_pieces(j, source, dots_row.at[me_r], dots_row, d1_send, d1_recv, "row")

    def d2_copy(j, source):
        return send_pieces(j, source, dots_col.at[me_c], dots_col, d2_send, d2_recv, "col")

    def start_gather():
        for t in range(own_tiles):
            piece = dir_ref[:, 128 * t : 128 * (t + 1)].astype(jnp.bfloat16)
            x_col[me_r * own_tiles + t] = piece
            x_row[me_c * own_tiles + t] = piece
        for d in far_first:
            gather_row(at_chip(d, core), me_r, at_chip(d, core)).start()
        gather_row(sibling, me_r, sibling).start()
        each_partner(n_col, me_c, lambda j: gather_col(j, me_c).start())

    def pass_row_on():
        for d in reversed(far_first):
            source = at_chip(d, core)
            gather_row(source, source, source).wait_recv()
            gather_row(sibling, source, at_chip(d, 1 - core)).start()
        gather_row(sibling, sibling, sibling).wait_recv()
        for d in reversed(far_first):
            source = at_chip(d, 1 - core)
            gather_row(sibling, source, source).wait_recv()

    def end_gather_sends():
        for d in far_first:
            gather_row(at_chip(d, core), me_r, at_chip(d, core)).wait_send()
            gather_row(sibling, at_chip(d, core), at_chip(d, 1 - core)).wait_send()
        gather_row(sibling, me_r, sibling).wait_send()
        all_cols.wait_send()

    def forward_tile(row, weigh):
        fields, weights = [], []
        for i in range(PER_ROW):
            code = row_table[0, row * PER_ROW + i]
            fields.append(weigh(x_col, code & 63, col_tiles))
            weights.append(tiles[code >> 6])
        return lax.dot_general(
            jnp.concatenate(fields, axis=1), jnp.concatenate(weights, axis=1),
            (((1,), (1,)), ((), ())), preferred_element_type=jnp.float32)

    def backward_tile(col, weigh):
        fields, weights = [], []
        for i in range(per_col):
            code = col_table[0, col * per_col + i]
            fields.append(weigh(x_row, code & 127, row_tiles))
            weights.append(tiles[code >> 7])
        return jnp.dot(
            jnp.concatenate(fields, axis=1), jnp.concatenate(weights, axis=0),
            preferred_element_type=jnp.float32)

    def field_of(x_ref, index, limit):
        return x_ref[index]

    def field_and_ones(x_ref, index, limit):
        unit = ones[jnp.where(index == limit, 1, 0)]
        return jnp.concatenate([x_ref[index], unit], axis=0)

    start_gather()
    live = count[0, 0]
    row_codes[...] = slot_table(rows[...], cols[...], live, PER_ROW, 6, col_tiles)
    col_codes[...] = slot_table(cols[...], rows[...], live, per_col, 7, row_tiles)
    table_copies = (
        pltpu.make_async_copy(row_codes, row_table, table_sem.at[0]),
        pltpu.make_async_copy(col_codes, col_table, table_sem.at[1]),
    )
    for copy in table_copies:
        copy.start()
    for i in range(tile_sem.shape[0]):
        tile_copy(i).wait()

    for copy in table_copies:
        copy.wait()

    def chunk_products(j, tile_of, part, first, d_part):
        for t in range(own_tiles):
            product = tile_of(j * own_tiles + t, field_and_ones if first else field_of)
            part[j * own_tiles + t] = product[:tasks].astype(part.dtype)
            if first:
                d_part[j, t : t + 1, :] = product[tasks : tasks + 1]
        if first:
            d_part[j, own_tiles:, :] = jnp.zeros((8 - own_tiles, 128), jnp.float32)

    def forward_products(first):
        def two(i, carry):
            for k in (2 * i, 2 * i + 1):
                chunk_products(partner(me_c, k, n_col), forward_tile, f_part, first, df_part)
            for k in (2 * i, 2 * i + 1):

                @pl.when(k != own_turn(n_col))
                def _(k=k):
                    j = partner(me_c, k, n_col)
                    f_send(j, me_c).start()
                    if first:
                        df_send(j, me_c).start()
            return carry

        lax.fori_loop(0, n_col // 2, two, 0)

    turns = far_first + [0]
    ahead = [(d, 0) for d in turns]
    behind = [(d, 1) for d in turns]
    order = [ahead[0]]
    for i in range(1, chips):
        order += [ahead[i], behind[i - 1]]
    order.append(behind[-1])

    def backward_products(first):
        def turn(k):
            d = pick(k, [d for d, final in order])
            final = pick(k, [final for d, final in order])
            return d, final, at_chip(d, core + (1 - final) * (1 - 2 * core))

        def two(i, carry):
            for k in (2 * i, 2 * i + 1):
                d, final, j = turn(k)
                chunk_products(j, backward_tile, b_part, first, db_part)
            for k in (2 * i, 2 * i + 1):
                d, final, j = turn(k)

                @pl.when(final == 0)
                def _(d=d):
                    pair_copy(d).start()

                @pl.when(final == 1)
                def _(d=d, j=j):
                    pair_copy(d).wait_recv()
                    for t in range(own_tiles):
                        b_part[j * own_tiles + t] = b_part[j * own_tiles + t] + pair[d, t]

                    @pl.when(d != 0)
                    def _():
                        b_send(d).start()

                if first:

                    @pl.when(j != me_r)
                    def _(j=j):
                        db_send(j, me_r).start()
            return carry

        lax.fori_loop(0, n_row // 2, two, 0)

    def gather_sums(n, own, send, recv, totals):
        def one(k, sums):
            j = (own + 1 + k) & (n - 1)
            send(j, j).wait_recv()
            return tuple(s + recv[j, t].astype(jnp.float32) for t, s in enumerate(sums))

        return lax.fori_loop(0, n - 1, one, totals)

    lane = lax.broadcasted_iota(jnp.int32, (tasks, 128), 1)
    task = lax.broadcasted_iota(jnp.int32, (tasks, 128), 0)

    def one_step(step, first):
        pass_row_on()
        forward_products(first)
        all_cols.wait_recv()
        backward_products(first)
        end_gather_sends()

        if first:
            df_recv[me_c] = df_part[me_c]
            db_recv[me_r] = db_part[me_r]
            all_df.wait_recv()
            all_db.wait_recv()
            total = sum(df_recv[i] for i in range(n_col)) + sum(db_recv[i] for i in range(n_row))
            degree[...] = 0.5 * total

        totals = tuple(
            f_part[me_c * own_tiles + t].astype(jnp.float32)
            + b_part[me_r * own_tiles + t].astype(jnp.float32)
            for t in range(own_tiles))
        totals = gather_sums(n_col, me_c, f_send, f_recv, totals)
        for d in reversed(far_first):
            b_arrival(d).wait_recv()
            source = (y + d) & (chips - 1)
            totals = tuple(s + b_recv[source, t] for t, s in enumerate(totals))

        pq = jnp.zeros((tasks, 128), jnp.float32)
        rq, qq, rr = pq, pq, pq
        images = []
        for t in range(own_tiles):
            part = slice(128 * t, 128 * (t + 1))
            p, r = dir_ref[:, part], res[:, part]
            q = p + coupling * (degree[t : t + 1, :] * p - 0.5 * totals[t])
            images.append(q)
            pq, rq, qq, rr = pq + p * q, rq + r * q, qq + q * q, rr + r * r
        row = jnp.zeros((tasks, 128), jnp.float32)
        for i, s in enumerate((pq, rq, qq, rr)):
            row = jnp.where(lane == task + tasks * i, jnp.sum(s, axis=1, keepdims=True), row)
        row = jnp.sum(row, axis=0, keepdims=True)
        dots_row[me_r] = row
        each_partner(n_row, me_r, lambda j: d1_copy(j, me_r).start())
        all_d1.wait_recv()
        dots_col[me_c] = sum(dots_row[i] for i in range(n_row))
        each_partner(n_col, me_c, lambda j: d2_copy(j, me_c).start())
        all_d2.wait_recv()
        sums = jnp.broadcast_to(sum(dots_col[i] for i in range(n_col)), (tasks, 128))
        pq, rq, qq, rr = (
            jnp.sum(jnp.where(lane == task + tasks * i, sums, 0.0), axis=1, keepdims=True)
            for i in range(4))
        size = rr / pq
        new = jnp.maximum(rr - 2.0 * size * rq + size * size * qq, 0.0)
        ratio = new / rr
        moves = []
        for t in range(own_tiles):
            part = slice(128 * t, 128 * (t + 1))
            p = dir_ref[:, part]
            r = res[:, part] - size * images[t]
            moves.append(size * p)
            res[:, part] = r
            dir_ref[:, part] = r + ratio * p

        @pl.when(step + 1 < ITERS)
        def _():
            start_gather()

        for t in range(own_tiles):
            part = slice(128 * t, 128 * (t + 1))
            sol[:, part] = sol[:, part] + moves[t]
        all_f.wait_send()
        for d in range(chips):
            pair_copy(d).wait_send()
        for d in far_first:
            b_send(d).wait_send()
        all_d1.wait_send()
        all_d2.wait_send()
        if first:
            all_df.wait_send()
            all_db.wait_send()

    one_step(0, True)

    def later_step(step, carry):
        one_step(step, False)
        return carry

    lax.fori_loop(1, ITERS, later_step, 0)


def per_device(n_row, n_col, scores, tile_values, tile_rows, tile_cols, tile_count):
    tiles = tile_values[0, 0]
    rows, cols = tile_rows[0], tile_cols[0]
    slots = tiles.shape[0]
    tasks, piece = scores.shape
    own_tiles = piece // 128
    row_tiles, col_tiles = own_tiles * n_col, own_tiles * n_row
    per_col = slots // col_tiles
    f32 = jnp.float32
    dma = pltpu.SemaphoreType.DMA
    vmem = pl.BlockSpec(memory_space=pltpu.VMEM)
    smem = pl.BlockSpec(memory_space=pltpu.SMEM)
    sol, res = pl.pallas_call(
        functools.partial(cg_kernel, n_row, n_col, per_col),
        out_shape=(
            jax.ShapeDtypeStruct((tasks, piece), f32),
            jax.ShapeDtypeStruct((tasks, piece), f32),
        ),
        in_specs=[smem, vmem, vmem, vmem, pl.BlockSpec(memory_space=pl.ANY)],
        out_specs=(vmem, vmem),
        scratch_shapes=[
            pltpu.VMEM((slots, 128, 128), jnp.bfloat16),
            pltpu.VMEM((col_tiles + 1, tasks, 128), jnp.bfloat16),
            pltpu.VMEM((row_tiles + 1, tasks, 128), jnp.bfloat16),
            pltpu.VMEM((row_tiles, tasks, 128), F_TYPE),
            pltpu.VMEM((col_tiles, tasks, 128), B_TYPE),
            pltpu.VMEM((n_col, own_tiles, tasks, 128), F_TYPE),
            pltpu.VMEM((n_row // 2, own_tiles, tasks, 128), B_TYPE),
            pltpu.VMEM((n_row // 2, own_tiles, tasks, 128), B_TYPE),
            pltpu.VMEM((n_col, 8, 128), f32),
            pltpu.VMEM((n_row, 8, 128), f32),
            pltpu.VMEM((n_col, 8, 128), f32),
            pltpu.VMEM((n_row, 8, 128), f32),
            pltpu.VMEM((2, 16, 128), jnp.bfloat16),
            pltpu.VMEM((tasks, piece), f32),
            pltpu.VMEM((8, 128), f32),
            pltpu.VMEM((n_row, 1, 128), f32),
            pltpu.VMEM((n_col, 1, 128), f32),
            pltpu.VMEM((1, slots), jnp.int32),
            pltpu.VMEM((1, slots), jnp.int32),
            pltpu.SMEM((1, slots), jnp.int32),
            pltpu.SMEM((1, slots), jnp.int32),
            dma((8,)), dma((2,)),
            dma((n_row,)), dma((n_row,)), dma((1,)), dma((1,)),
            dma((1,)), dma((n_col,)), dma((n_row // 2,)), dma((n_row // 2,)),
            dma((n_row // 2,)), dma((n_row // 2,)),
            dma((1,)), dma((1,)), dma((1,)), dma((1,)),
            dma((1,)), dma((1,)), dma((1,)), dma((1,)),
        ],
        compiler_params=pltpu.CompilerParams(
            collective_id=0, has_side_effects=True, vmem_limit_bytes=56 * 1024 * 1024
        ),
    )(tile_count, rows, cols, scores, tiles)
    return pl.pallas_call(
        copy_kernel,
        out_shape=(
            jax.ShapeDtypeStruct((tasks, piece), f32),
            jax.ShapeDtypeStruct((tasks, piece), f32),
        ),
        in_specs=[vmem, vmem],
        out_specs=(vmem, vmem),
    )(sol, res)


def solution(mesh):
    return jax.shard_map(
        functools.partial(per_device, mesh.shape["row"], mesh.shape["col"]),
        mesh=mesh,
        in_specs=(
            P(None, ("row", "col")),
            P("row", "col", None, None, None),
            P("row", "col", None),
            P("row", "col", None),
            P("row", "col"),
        ),
        out_specs=(P(None, ("row", "col")), P(None, ("row", "col"))),
        check_vma=False,
    )
```

```python
import functools

import jax
import jax.numpy as jnp
from jax import lax
from jax.experimental import pallas as pl
from jax.experimental.pallas import tpu as pltpu
from jax.sharding import PartitionSpec as P

PER_ROW = 5
ITERS = 3
MESH = pl.DeviceIdType.MESH
F_TYPE = jnp.bfloat16
B_TYPE = jnp.float32

coupling = 0.2


def spread(n):
    fast = 2 if n <= 8 else 4
    return n // fast, fast


def partner(me, k, n):
    slow, fast = spread(n)
    bits = fast.bit_length() - 1
    a = ((me >> bits) + slow // 2 + (k >> bits)) & (slow - 1)
    b = (me + fast // 2 + k) & (fast - 1)
    return a * fast + b


def own_turn(n):
    slow, fast = spread(n)
    return (slow - slow // 2) % slow * fast + (fast - fast // 2) % fast


def slot_table(own, other, live, per_tile, shift, empty):
    n = own.shape[1]
    here = lax.broadcasted_iota(jnp.int32, (n, n), 0)
    there = lax.broadcasted_iota(jnp.int32, (n, n), 1)

    def down(line):
        return jnp.sum(jnp.where(here == there, line, 0), axis=1, keepdims=True)

    own_down, other_down = down(own), down(other)
    earlier = (own_down == own) & (there < here)
    key = own_down * per_tile + jnp.sum(jnp.where(earlier, 1, 0), axis=1, keepdims=True)
    slot = here[:, :1]
    code = (slot << shift) + jnp.where(slot < live, other_down, empty)
    return jnp.sum(jnp.where(key == there, code, 0), axis=0, keepdims=True)


def copy_kernel(sol_in, res_in, sol, res):
    sol[...] = sol_in[...]
    res[...] = res_in[...]


def pick(index, values):
    value = values[-1]
    for i, v in enumerate(values[:-1]):
        value = jnp.where(index == i, v, value)
    return value


def cg_kernel(
    n_row, n_col, per_col,
    count, rows, cols, scores, tiles_hbm, sol, res,
    tiles, x_col, x_row, f_part, b_part, f_recv, b_recv, pair,
    df_part, db_part, df_recv, db_recv, ones, dir_ref, degree, dots_row, dots_col,
    row_codes, col_codes, row_table, col_table,
    tile_sem, table_sem,
    agr_send, agr_recv, agc_send, agc_recv, first_x, first_z,
    rsf_send, rsf_recv, rsb_send, rsb_recv, pair_send, pair_recv,
    dgf_send, dgf_recv, dgb_send, dgb_recv,
    d1_send, d1_recv, d2_send, d2_recv,
):
    me_r = lax.axis_index("row")
    me_c = lax.axis_index("col")
    y, core = me_r >> 1, me_r & 1
    chips = n_row // 2
    sibling = me_r + 1 - 2 * core
    side_x, side_z = spread(n_col)
    x, z = me_c // side_z, me_c % side_z

    def by_distance(side):
        return sorted(range(1, side), key=lambda d: -min(d, side - d))

    far_first, far_x, far_z = by_distance(chips), by_distance(side_x), by_distance(side_z)
    tasks = scores.shape[0]
    own_tiles = scores.shape[1] // 128
    half = own_tiles // 2
    slots = tiles.shape[0]
    col_tiles = b_part.shape[0]
    row_tiles = f_part.shape[0]
    chunk = slots // tile_sem.shape[0]

    def tile_copy(i):
        part = pl.ds(i * chunk, chunk)
        return pltpu.make_async_copy(tiles_hbm.at[part], tiles.at[part], tile_sem.at[i])

    for i in range(tile_sem.shape[0]):
        tile_copy(i).start()

    barrier = pltpu.get_barrier_semaphore()

    def greet(axis, n, own):
        def one(k, carry):
            @pl.when(k != own_turn(n))
            def _():
                j = partner(own, k, n)
                target = (me_r, j) if axis == "col" else (j, me_c)
                pl.semaphore_signal(barrier, inc=1, device_id=target, device_id_type=MESH)
            return carry

        lax.fori_loop(0, n, one, 0)

    greet("col", n_col, me_c)
    greet("row", n_row, me_r)

    x_col[col_tiles] = jnp.zeros((tasks, 128), jnp.bfloat16)
    x_row[row_tiles] = jnp.zeros((tasks, 128), jnp.bfloat16)
    ones[0] = jnp.ones((16, 128), jnp.bfloat16)
    ones[1] = jnp.zeros((16, 128), jnp.bfloat16)
    dir_ref[...] = scores[...]
    res[...] = scores[...]
    sol[...] = jnp.zeros_like(sol)

    pl.semaphore_wait(barrier, n_row + n_col - 2)

    def each_partner(n, own, action):
        def one(k, carry):
            @pl.when(k != own_turn(n))
            def _():
                action(partner(own, k, n))
            return carry

        lax.fori_loop(0, n, one, 0)

    own_col = pl.ds(me_r * own_tiles, own_tiles)
    own_row = pl.ds(me_c * own_tiles, own_tiles)

    def gather_row(j, source, sem):
        part = pl.ds(source * own_tiles, own_tiles)
        return pltpu.make_async_remote_copy(
            src_ref=x_col.at[part], dst_ref=x_col.at[part],
            send_sem=agr_send.at[sem], recv_sem=agr_recv.at[source],
            device_id=(j, me_c), device_id_type=MESH,
        )

    def all_of(ref, number, send_sem, recv_sem):
        part = ref.at[pl.ds(0, number)]
        return pltpu.make_async_remote_copy(
            src_ref=part, dst_ref=part, send_sem=send_sem.at[0], recv_sem=recv_sem.at[0],
            device_id=(sibling, me_c), device_id_type=MESH,
        )

    others_row, others_col = n_row - 1, n_col - 1
    all_cols = all_of(x_row, others_col * own_tiles, agc_send, agc_send)
    second = half * (side_x * (side_z - 1) + side_z * (side_x - 1))
    second_phase = all_of(x_row, second, agc_recv, agc_recv)
    all_f = all_of(f_part, others_col * own_tiles, rsf_send, rsf_send)
    all_df = all_of(df_recv, others_col, dgf_send, dgf_recv)
    all_db = all_of(db_recv, others_row, dgb_send, dgb_recv)
    all_d1 = all_of(dots_row, others_row, d1_send, d1_recv)
    all_d2 = all_of(dots_col, others_col, d2_send, d2_recv)

    def at_chip(d, on_core):
        return ((y + d) & (chips - 1)) * 2 + on_core

    def at_place(dx, dz):
        return ((x + dx) & (side_x - 1)) * side_z + ((z + dz) & (side_z - 1))

    def gather_half(target, source, which, recv_sem):
        part = pl.ds(source * own_tiles + which * half, half)
        return pltpu.make_async_remote_copy(
            src_ref=x_row.at[part], dst_ref=x_row.at[part],
            send_sem=agc_send.at[0], recv_sem=recv_sem,
            device_id=(me_r, target), device_id_type=MESH,
        )

    def start_cols():
        for d in far_x:
            gather_half(at_place(d, 0), me_c, 0, first_x.at[x]).start()
        for d in far_z:
            gather_half(at_place(0, d), me_c, 1, first_z.at[z]).start()
        pass_x_on(0)
        pass_z_on(0)

    def pass_x_on(dx):
        source = at_place(dx, 0)
        if dx:
            gather_half(source, source, 0, first_x.at[(x + dx) & (side_x - 1)]).wait_recv()
        for d in far_z:
            gather_half(at_place(0, d), source, 0, agc_recv.at[0]).start()

    def pass_z_on(dz):
        source = at_place(0, dz)
        if dz:
            gather_half(source, source, 1, first_z.at[(z + dz) & (side_z - 1)]).wait_recv()
        for d in far_x:
            gather_half(at_place(d, 0), source, 1, agc_recv.at[0]).start()

    def send_pieces(j, source, part, recv, send_sem, recv_sem, axis):
        return pltpu.make_async_remote_copy(
            src_ref=part, dst_ref=recv.at[source],
            send_sem=send_sem.at[0], recv_sem=recv_sem.at[source if recv is f_recv else 0],
            device_id=(me_r, j) if axis == "col" else (j, me_c), device_id_type=MESH,
        )

    def f_send(j, source):
        return send_pieces(
            j, source, f_part.at[pl.ds(j * own_tiles, own_tiles)], f_recv, rsf_send, rsf_recv, "col")

    def b_send(d):
        j = at_chip(d, core)
        return pltpu.make_async_remote_copy(
            src_ref=b_part.at[pl.ds(j * own_tiles, own_tiles)], dst_ref=b_recv.at[y],
            send_sem=rsb_send.at[d], recv_sem=rsb_recv.at[y],
            device_id=(j, me_c), device_id_type=MESH,
        )

    def b_arrival(d):
        source = (y + d) & (chips - 1)
        return pltpu.make_async_remote_copy(
            src_ref=b_part.at[pl.ds(me_r * own_tiles, own_tiles)], dst_ref=b_recv.at[source],
            send_sem=rsb_send.at[d], recv_sem=rsb_recv.at[source],
            device_id=(at_chip(d, core), me_c), device_id_type=MESH,
        )

    def pair_copy(d):
        j = at_chip(d, 1 - core)
        return pltpu.make_async_remote_copy(
            src_ref=b_part.at[pl.ds(j * own_tiles, own_tiles)], dst_ref=pair.at[d],
            send_sem=pair_send.at[d], recv_sem=pair_recv.at[d],
            device_id=(sibling, me_c), device_id_type=MESH,
        )

    def df_send(j, source):
        return send_pieces(j, source, df_part.at[j], df_recv, dgf_send, dgf_recv, "col")

    def db_send(j, source):
        return send_pieces(j, source, db_part.at[j], db_recv, dgb_send, dgb_recv, "row")

    def d1_copy(j, source):
        return send_pieces(j, source, dots_row.at[me_r], dots_row, d1_send, d1_recv, "row")

    def d2_copy(j, source):
        return send_pieces(j, source, dots_col.at[me_c], dots_col, d2_send, d2_recv, "col")

    def start_gather():
        for t in range(own_tiles):
            piece = dir_ref[:, 128 * t : 128 * (t + 1)].astype(jnp.bfloat16)
            x_col[me_r * own_tiles + t] = piece
            x_row[me_c * own_tiles + t] = piece
        for d in far_first:
            gather_row(at_chip(d, core), me_r, at_chip(d, core)).start()
        gather_row(sibling, me_r, sibling).start()
        start_cols()

    def pass_y_on(d):
        source = at_chip(d, core)
        gather_row(source, source, source).wait_recv()
        gather_row(sibling, source, at_chip(d, 1 - core)).start()

    def pass_on():
        for d in reversed(far_first[1:]):
            pass_y_on(d)
        for d in reversed(far_x[1:]):
            pass_x_on(d)
        for d in reversed(far_z[1:]):
            pass_z_on(d)
        pass_y_on(far_first[0])
        pass_x_on(far_x[0])
        pass_z_on(far_z[0])
        gather_row(sibling, sibling, sibling).wait_recv()
        for d in reversed(far_first):
            source = at_chip(d, 1 - core)
            gather_row(sibling, source, source).wait_recv()

    def end_gather_sends():
        for d in far_first:
            gather_row(at_chip(d, core), me_r, at_chip(d, core)).wait_send()
            gather_row(sibling, at_chip(d, core), at_chip(d, 1 - core)).wait_send()
        gather_row(sibling, me_r, sibling).wait_send()
        all_cols.wait_send()

    def wide_dot(fields, weights):
        return lax.dot_general(
            fields, jnp.concatenate(weights, axis=1),
            (((1,), (1,)), ((), ())), preferred_element_type=jnp.float32)

    def forward_tiles(row, weigh):
        sums, last_fields, last_weights = [], [], []
        for r in (row, row + 1):
            fields, weights = [], []
            for i in range(PER_ROW):
                code = row_table[0, r * PER_ROW + i]
                fields.append(weigh(x_col, code & 63, col_tiles))
                weights.append(tiles[code >> 6])
            sums.append(wide_dot(jnp.concatenate(fields[:-1], axis=1), weights[:-1]))
            last_fields.append(fields[-1])
            last_weights.append(weights[-1])
        zeros = jnp.zeros_like(last_fields[0])
        lines = jnp.concatenate([
            jnp.concatenate([last_fields[0], zeros], axis=1),
            jnp.concatenate([zeros, last_fields[1]], axis=1)], axis=0)
        last = wide_dot(lines, last_weights)
        height = zeros.shape[0]
        return [sums[0] + last[:height], sums[1] + last[height:]]

    def backward_tiles(col, weigh):
        return [backward_tile(col, weigh), backward_tile(col + 1, weigh)]

    def backward_tile(col, weigh):
        fields, weights = [], []
        for i in range(per_col):
            code = col_table[0, col * per_col + i]
            fields.append(weigh(x_row, code & 127, row_tiles))
            weights.append(tiles[code >> 7])
        return jnp.dot(
            jnp.concatenate(fields, axis=1), jnp.concatenate(weights, axis=0),
            preferred_element_type=jnp.float32)

    def field_of(x_ref, index, limit):
        return x_ref[index]

    def field_and_ones(x_ref, index, limit):
        unit = ones[jnp.where(index == limit, 1, 0)]
        return jnp.concatenate([x_ref[index], unit], axis=0)

    start_gather()
    live = count[0, 0]
    row_codes[...] = slot_table(rows[...], cols[...], live, PER_ROW, 6, col_tiles)
    col_codes[...] = slot_table(cols[...], rows[...], live, per_col, 7, row_tiles)
    table_copies = (
        pltpu.make_async_copy(row_codes, row_table, table_sem.at[0]),
        pltpu.make_async_copy(col_codes, col_table, table_sem.at[1]),
    )
    for copy in table_copies:
        copy.start()
    for i in range(tile_sem.shape[0]):
        tile_copy(i).wait()

    for copy in table_copies:
        copy.wait()

    def chunk_products(j, tiles_of, part, first, d_part):
        for t in range(0, own_tiles, 2):
            products = tiles_of(j * own_tiles + t, field_and_ones if first else field_of)
            for i, product in enumerate(products):
                part[j * own_tiles + t + i] = product[:tasks].astype(part.dtype)
                if first:
                    d_part[j, t + i : t + i + 1, :] = product[tasks : tasks + 1]
        if first:
            d_part[j, own_tiles:, :] = jnp.zeros((8 - own_tiles, 128), jnp.float32)

    def forward_products(first):
        def two(i, carry):
            for k in (2 * i, 2 * i + 1):
                chunk_products(partner(me_c, k, n_col), forward_tiles, f_part, first, df_part)
            for k in (2 * i, 2 * i + 1):

                @pl.when(k != own_turn(n_col))
                def _(k=k):
                    j = partner(me_c, k, n_col)
                    f_send(j, me_c).start()
                    if first:
                        df_send(j, me_c).start()
            return carry

        lax.fori_loop(0, n_col // 2, two, 0)

    turns = far_first + [0]
    ahead = [(d, 0) for d in turns]
    behind = [(d, 1) for d in turns]
    order = ahead[:-1] + behind[:-1] + [ahead[-1], behind[-1]]

    def backward_products(first):
        def turn(k):
            d = pick(k, [d for d, final in order])
            final = pick(k, [final for d, final in order])
            return d, final, at_chip(d, core + (1 - final) * (1 - 2 * core))

        def two(i, carry):
            for k in (2 * i, 2 * i + 1):
                d, final, j = turn(k)
                chunk_products(j, backward_tiles, b_part, first, db_part)
            for k in (2 * i, 2 * i + 1):
                d, final, j = turn(k)

                @pl.when(final == 0)
                def _(d=d):
                    pair_copy(d).start()

                @pl.when(final == 1)
                def _(d=d, j=j):
                    pair_copy(d).wait_recv()
                    for t in range(own_tiles):
                        b_part[j * own_tiles + t] = b_part[j * own_tiles + t] + pair[d, t]

                    @pl.when(d != 0)
                    def _():
                        b_send(d).start()

                if first:

                    @pl.when(j != me_r)
                    def _(j=j):
                        db_send(j, me_r).start()
            return carry

        lax.fori_loop(0, n_row // 2, two, 0)

    def gather_sums(n, own, send, recv, totals):
        def one(k, sums):
            j = (own + 1 + k) & (n - 1)
            send(j, j).wait_recv()
            return tuple(s + recv[j, t].astype(jnp.float32) for t, s in enumerate(sums))

        return lax.fori_loop(0, n - 1, one, totals)

    lane = lax.broadcasted_iota(jnp.int32, (tasks, 128), 1)
    task = lax.broadcasted_iota(jnp.int32, (tasks, 128), 0)

    def one_step(step, first):
        pass_on()
        forward_products(first)
        second_phase.wait_recv()
        backward_products(first)
        end_gather_sends()

        if first:
            df_recv[me_c] = df_part[me_c]
            db_recv[me_r] = db_part[me_r]
            all_df.wait_recv()
            all_db.wait_recv()
            total = sum(df_recv[i] for i in range(n_col)) + sum(db_recv[i] for i in range(n_row))
            degree[...] = 0.5 * total

        totals = tuple(
            f_part[me_c * own_tiles + t].astype(jnp.float32)
            + b_part[me_r * own_tiles + t].astype(jnp.float32)
            for t in range(own_tiles))
        totals = gather_sums(n_col, me_c, f_send, f_recv, totals)
        for d in reversed(far_first):
            b_arrival(d).wait_recv()
            source = (y + d) & (chips - 1)
            totals = tuple(s + b_recv[source, t] for t, s in enumerate(totals))

        pq = jnp.zeros((tasks, 128), jnp.float32)
        rq, qq, rr = pq, pq, pq
        images = []
        for t in range(own_tiles):
            part = slice(128 * t, 128 * (t + 1))
            p, r = dir_ref[:, part], res[:, part]
            q = p + coupling * (degree[t : t + 1, :] * p - 0.5 * totals[t])
            images.append(q)
            pq, rq, qq, rr = pq + p * q, rq + r * q, qq + q * q, rr + r * r
        row = jnp.zeros((tasks, 128), jnp.float32)
        for i, s in enumerate((pq, rq, qq, rr)):
            row = jnp.where(lane == task + tasks * i, jnp.sum(s, axis=1, keepdims=True), row)
        row = jnp.sum(row, axis=0, keepdims=True)
        dots_row[me_r] = row
        each_partner(n_row, me_r, lambda j: d1_copy(j, me_r).start())
        all_d1.wait_recv()
        dots_col[me_c] = sum(dots_row[i] for i in range(n_row))
        each_partner(n_col, me_c, lambda j: d2_copy(j, me_c).start())
        all_d2.wait_recv()
        sums = jnp.broadcast_to(sum(dots_col[i] for i in range(n_col)), (tasks, 128))
        pq, rq, qq, rr = (
            jnp.sum(jnp.where(lane == task + tasks * i, sums, 0.0), axis=1, keepdims=True)
            for i in range(4))
        size = rr / pq
        new = jnp.maximum(rr - 2.0 * size * rq + size * size * qq, 0.0)
        ratio = new / rr
        moves = []
        for t in range(own_tiles):
            part = slice(128 * t, 128 * (t + 1))
            p = dir_ref[:, part]
            r = res[:, part] - size * images[t]
            moves.append(size * p)
            res[:, part] = r
            dir_ref[:, part] = r + ratio * p

        @pl.when(step + 1 < ITERS)
        def _():
            start_gather()

        for t in range(own_tiles):
            part = slice(128 * t, 128 * (t + 1))
            sol[:, part] = sol[:, part] + moves[t]
        all_f.wait_send()
        for d in range(chips):
            pair_copy(d).wait_send()
        for d in far_first:
            b_send(d).wait_send()
        all_d1.wait_send()
        all_d2.wait_send()
        if first:
            all_df.wait_send()
            all_db.wait_send()

    one_step(0, True)

    def later_step(step, carry):
        one_step(step, False)
        return carry

    lax.fori_loop(1, ITERS, later_step, 0)


def per_device(n_row, n_col, scores, tile_values, tile_rows, tile_cols, tile_count):
    tiles = tile_values[0, 0]
    rows, cols = tile_rows[0], tile_cols[0]
    slots = tiles.shape[0]
    tasks, piece = scores.shape
    own_tiles = piece // 128
    row_tiles, col_tiles = own_tiles * n_col, own_tiles * n_row
    per_col = slots // col_tiles
    f32 = jnp.float32
    dma = pltpu.SemaphoreType.DMA
    vmem = pl.BlockSpec(memory_space=pltpu.VMEM)
    smem = pl.BlockSpec(memory_space=pltpu.SMEM)
    sol, res = pl.pallas_call(
        functools.partial(cg_kernel, n_row, n_col, per_col),
        out_shape=(
            jax.ShapeDtypeStruct((tasks, piece), f32),
            jax.ShapeDtypeStruct((tasks, piece), f32),
        ),
        in_specs=[smem, vmem, vmem, vmem, pl.BlockSpec(memory_space=pl.ANY)],
        out_specs=(vmem, vmem),
        scratch_shapes=[
            pltpu.VMEM((slots, 128, 128), jnp.bfloat16),
            pltpu.VMEM((col_tiles + 1, tasks, 128), jnp.bfloat16),
            pltpu.VMEM((row_tiles + 1, tasks, 128), jnp.bfloat16),
            pltpu.VMEM((row_tiles, tasks, 128), F_TYPE),
            pltpu.VMEM((col_tiles, tasks, 128), B_TYPE),
            pltpu.VMEM((n_col, own_tiles, tasks, 128), F_TYPE),
            pltpu.VMEM((n_row // 2, own_tiles, tasks, 128), B_TYPE),
            pltpu.VMEM((n_row // 2, own_tiles, tasks, 128), B_TYPE),
            pltpu.VMEM((n_col, 8, 128), f32),
            pltpu.VMEM((n_row, 8, 128), f32),
            pltpu.VMEM((n_col, 8, 128), f32),
            pltpu.VMEM((n_row, 8, 128), f32),
            pltpu.VMEM((2, 16, 128), jnp.bfloat16),
            pltpu.VMEM((tasks, piece), f32),
            pltpu.VMEM((8, 128), f32),
            pltpu.VMEM((n_row, 1, 128), f32),
            pltpu.VMEM((n_col, 1, 128), f32),
            pltpu.VMEM((1, slots), jnp.int32),
            pltpu.VMEM((1, slots), jnp.int32),
            pltpu.SMEM((1, slots), jnp.int32),
            pltpu.SMEM((1, slots), jnp.int32),
            dma((8,)), dma((2,)),
            dma((n_row,)), dma((n_row,)), dma((1,)), dma((1,)),
            dma((spread(n_col)[0],)), dma((spread(n_col)[1],)),
            dma((1,)), dma((n_col,)), dma((n_row // 2,)), dma((n_row // 2,)),
            dma((n_row // 2,)), dma((n_row // 2,)),
            dma((1,)), dma((1,)), dma((1,)), dma((1,)),
            dma((1,)), dma((1,)), dma((1,)), dma((1,)),
        ],
        compiler_params=pltpu.CompilerParams(
            collective_id=0, has_side_effects=True, vmem_limit_bytes=56 * 1024 * 1024
        ),
    )(tile_count, rows, cols, scores, tiles)
    return pl.pallas_call(
        copy_kernel,
        out_shape=(
            jax.ShapeDtypeStruct((tasks, piece), f32),
            jax.ShapeDtypeStruct((tasks, piece), f32),
        ),
        in_specs=[vmem, vmem],
        out_specs=(vmem, vmem),
    )(sol, res)


def solution(mesh):
    return jax.shard_map(
        functools.partial(per_device, mesh.shape["row"], mesh.shape["col"]),
        mesh=mesh,
        in_specs=(
            P(None, ("row", "col")),
            P("row", "col", None, None, None),
            P("row", "col", None),
            P("row", "col", None),
            P("row", "col"),
        ),
        out_specs=(P(None, ("row", "col")), P(None, ("row", "col"))),
        check_vma=False,
    )
```

```python
import functools

import jax
import jax.numpy as jnp
from jax import lax
from jax.experimental import pallas as pl
from jax.experimental.pallas import tpu as pltpu
from jax.sharding import PartitionSpec as P

PER_ROW = 5
ITERS = 3
MESH = pl.DeviceIdType.MESH
F_TYPE = jnp.bfloat16
B_TYPE = jnp.float32

coupling = 0.2


def spread(n):
    fast = 2 if n <= 8 else 4
    return n // fast, fast


def partner(me, k, n):
    slow, fast = spread(n)
    bits = fast.bit_length() - 1
    a = ((me >> bits) + slow // 2 + (k >> bits)) & (slow - 1)
    b = (me + fast // 2 + k) & (fast - 1)
    return a * fast + b


def own_turn(n):
    slow, fast = spread(n)
    return (slow - slow // 2) % slow * fast + (fast - fast // 2) % fast


def slot_table(own, other, live, per_tile, shift, empty):
    n = own.shape[1]
    here = lax.broadcasted_iota(jnp.int32, (n, n), 0)
    there = lax.broadcasted_iota(jnp.int32, (n, n), 1)

    def down(line):
        return jnp.sum(jnp.where(here == there, line, 0), axis=1, keepdims=True)

    own_down, other_down = down(own), down(other)
    earlier = (own_down == own) & (there < here)
    key = own_down * per_tile + jnp.sum(jnp.where(earlier, 1, 0), axis=1, keepdims=True)
    slot = here[:, :1]
    code = (slot << shift) + jnp.where(slot < live, other_down, empty)
    return jnp.sum(jnp.where(key == there, code, 0), axis=0, keepdims=True)


def copy_kernel(sol_in, res_in, sol, res):
    sol[...] = sol_in[...]
    res[...] = res_in[...]


def pick(index, values):
    value = values[-1]
    for i, v in enumerate(values[:-1]):
        value = jnp.where(index == i, v, value)
    return value


def cg_kernel(
    n_row, n_col, per_col,
    count, rows, cols, scores, tiles_hbm, sol, res,
    tiles, x_col, x_row, f_part, b_part, f_recv, b_recv, pair,
    df_part, db_part, df_recv, db_recv, ones, dir_ref, degree, dots_row, dots_col,
    row_codes, col_codes, row_table, col_table,
    tile_sem, table_sem,
    agr_send, agr_recv, agc_send, agc_recv, first_x, first_z,
    rsf_send, rsf_recv, rsb_send, rsb_recv, pair_send, pair_recv,
    dgf_send, dgf_recv, dgb_send, dgb_recv,
    d1_send, d1_recv, d2_send, d2_recv,
):
    me_r = lax.axis_index("row")
    me_c = lax.axis_index("col")
    y, core = me_r >> 1, me_r & 1
    chips = n_row // 2
    sibling = me_r + 1 - 2 * core
    side_x, side_z = spread(n_col)
    x, z = me_c // side_z, me_c % side_z

    def by_distance(side):
        return sorted(range(1, side), key=lambda d: -min(d, side - d))

    far_first, far_x, far_z = by_distance(chips), by_distance(side_x), by_distance(side_z)
    tasks = scores.shape[0]
    own_tiles = scores.shape[1] // 128
    half = own_tiles // 2
    slots = tiles.shape[0]
    col_tiles = b_part.shape[0]
    row_tiles = f_part.shape[0]
    chunk = slots // tile_sem.shape[0]

    def tile_copy(i):
        part = pl.ds(i * chunk, chunk)
        return pltpu.make_async_copy(tiles_hbm.at[part], tiles.at[part], tile_sem.at[i])

    for i in range(tile_sem.shape[0]):
        tile_copy(i).start()

    barrier = pltpu.get_barrier_semaphore()

    def greet(axis, n, own):
        def one(k, carry):
            @pl.when(k != own_turn(n))
            def _():
                j = partner(own, k, n)
                target = (me_r, j) if axis == "col" else (j, me_c)
                pl.semaphore_signal(barrier, inc=1, device_id=target, device_id_type=MESH)
            return carry

        lax.fori_loop(0, n, one, 0)

    greet("col", n_col, me_c)
    greet("row", n_row, me_r)

    x_col[col_tiles] = jnp.zeros((tasks, 128), jnp.bfloat16)
    x_row[row_tiles] = jnp.zeros((tasks, 128), jnp.bfloat16)
    ones[0] = jnp.ones((16, 128), jnp.bfloat16)
    ones[1] = jnp.zeros((16, 128), jnp.bfloat16)
    dir_ref[...] = scores[...]
    res[...] = scores[...]
    sol[...] = jnp.zeros_like(sol)

    pl.semaphore_wait(barrier, n_row + n_col - 2)

    def each_partner(n, own, action):
        def one(k, carry):
            @pl.when(k != own_turn(n))
            def _():
                action(partner(own, k, n))
            return carry

        lax.fori_loop(0, n, one, 0)

    own_col = pl.ds(me_r * own_tiles, own_tiles)
    own_row = pl.ds(me_c * own_tiles, own_tiles)

    def gather_row(j, source, sem):
        part = pl.ds(source * own_tiles, own_tiles)
        return pltpu.make_async_remote_copy(
            src_ref=x_col.at[part], dst_ref=x_col.at[part],
            send_sem=agr_send.at[sem], recv_sem=agr_recv.at[source],
            device_id=(j, me_c), device_id_type=MESH,
        )

    def all_of(ref, number, send_sem, recv_sem):
        part = ref.at[pl.ds(0, number)]
        return pltpu.make_async_remote_copy(
            src_ref=part, dst_ref=part, send_sem=send_sem.at[0], recv_sem=recv_sem.at[0],
            device_id=(sibling, me_c), device_id_type=MESH,
        )

    others_row, others_col = n_row - 1, n_col - 1
    all_cols = all_of(x_row, others_col * own_tiles, agc_send, agc_send)
    second = half * (side_x * (side_z - 1) + side_z * (side_x - 1))
    second_phase = all_of(x_row, second, agc_recv, agc_recv)
    all_f = all_of(f_part, others_col * own_tiles, rsf_send, rsf_send)
    all_df = all_of(df_recv, others_col, dgf_send, dgf_recv)
    all_db = all_of(db_recv, others_row, dgb_send, dgb_recv)
    all_d1 = all_of(dots_row, others_row, d1_send, d1_recv)
    all_d2 = all_of(dots_col, others_col, d2_send, d2_recv)

    def at_chip(d, on_core):
        return ((y + d) & (chips - 1)) * 2 + on_core

    def at_place(dx, dz):
        return ((x + dx) & (side_x - 1)) * side_z + ((z + dz) & (side_z - 1))

    def gather_half(target, source, which, recv_sem):
        part = pl.ds(source * own_tiles + which * half, half)
        return pltpu.make_async_remote_copy(
            src_ref=x_row.at[part], dst_ref=x_row.at[part],
            send_sem=agc_send.at[0], recv_sem=recv_sem,
            device_id=(me_r, target), device_id_type=MESH,
        )

    def start_cols():
        for d in far_x:
            gather_half(at_place(d, 0), me_c, 0, first_x.at[x]).start()
        for d in far_z:
            gather_half(at_place(0, d), me_c, 1, first_z.at[z]).start()
        pass_x_on(0)
        pass_z_on(0)

    def pass_x_on(dx):
        source = at_place(dx, 0)
        if dx:
            gather_half(source, source, 0, first_x.at[(x + dx) & (side_x - 1)]).wait_recv()
        for d in far_z:
            gather_half(at_place(0, d), source, 0, agc_recv.at[0]).start()

    def pass_z_on(dz):
        source = at_place(0, dz)
        if dz:
            gather_half(source, source, 1, first_z.at[(z + dz) & (side_z - 1)]).wait_recv()
        for d in far_x:
            gather_half(at_place(d, 0), source, 1, agc_recv.at[0]).start()

    def send_pieces(j, source, part, recv, send_sem, recv_sem, axis):
        return pltpu.make_async_remote_copy(
            src_ref=part, dst_ref=recv.at[source],
            send_sem=send_sem.at[0], recv_sem=recv_sem.at[source if recv is f_recv else 0],
            device_id=(me_r, j) if axis == "col" else (j, me_c), device_id_type=MESH,
        )

    def f_send(j, source):
        return send_pieces(
            j, source, f_part.at[pl.ds(j * own_tiles, own_tiles)], f_recv, rsf_send, rsf_recv, "col")

    def b_send(d):
        j = at_chip(d, core)
        return pltpu.make_async_remote_copy(
            src_ref=b_part.at[pl.ds(j * own_tiles, own_tiles)], dst_ref=b_recv.at[y],
            send_sem=rsb_send.at[d], recv_sem=rsb_recv.at[y],
            device_id=(j, me_c), device_id_type=MESH,
        )

    def b_arrival(d):
        source = (y + d) & (chips - 1)
        return pltpu.make_async_remote_copy(
            src_ref=b_part.at[pl.ds(me_r * own_tiles, own_tiles)], dst_ref=b_recv.at[source],
            send_sem=rsb_send.at[d], recv_sem=rsb_recv.at[source],
            device_id=(at_chip(d, core), me_c), device_id_type=MESH,
        )

    def pair_copy(d):
        j = at_chip(d, 1 - core)
        return pltpu.make_async_remote_copy(
            src_ref=b_part.at[pl.ds(j * own_tiles, own_tiles)], dst_ref=pair.at[d],
            send_sem=pair_send.at[d], recv_sem=pair_recv.at[d],
            device_id=(sibling, me_c), device_id_type=MESH,
        )

    def df_send(j, source):
        return send_pieces(j, source, df_part.at[j], df_recv, dgf_send, dgf_recv, "col")

    def db_send(j, source):
        return send_pieces(j, source, db_part.at[j], db_recv, dgb_send, dgb_recv, "row")

    def d1_copy(j, source):
        return send_pieces(j, source, dots_row.at[me_r], dots_row, d1_send, d1_recv, "row")

    def d2_copy(j, source):
        return send_pieces(j, source, dots_col.at[me_c], dots_col, d2_send, d2_recv, "col")

    def start_gather():
        for t in range(own_tiles):
            piece = dir_ref[:, 128 * t : 128 * (t + 1)].astype(jnp.bfloat16)
            x_col[me_r * own_tiles + t] = piece
            x_row[me_c * own_tiles + t] = piece
        for d in far_first:
            gather_row(at_chip(d, core), me_r, at_chip(d, core)).start()
        gather_row(sibling, me_r, sibling).start()
        start_cols()

    def pass_y_on(d):
        source = at_chip(d, core)
        gather_row(source, source, source).wait_recv()
        gather_row(sibling, source, at_chip(d, 1 - core)).start()

    def pass_on():
        for d in reversed(far_first[1:]):
            pass_y_on(d)
        for d in reversed(far_x[1:]):
            pass_x_on(d)
        for d in reversed(far_z[1:]):
            pass_z_on(d)
        pass_y_on(far_first[0])
        pass_x_on(far_x[0])
        pass_z_on(far_z[0])
        gather_row(sibling, sibling, sibling).wait_recv()
        for d in reversed(far_first):
            source = at_chip(d, 1 - core)
            gather_row(sibling, source, source).wait_recv()

    def end_gather_sends():
        for d in far_first:
            gather_row(at_chip(d, core), me_r, at_chip(d, core)).wait_send()
            gather_row(sibling, at_chip(d, core), at_chip(d, 1 - core)).wait_send()
        gather_row(sibling, me_r, sibling).wait_send()
        all_cols.wait_send()

    def wide_dot(fields, weights):
        return lax.dot_general(
            fields, jnp.concatenate(weights, axis=1),
            (((1,), (1,)), ((), ())), preferred_element_type=jnp.float32)

    def forward_tiles(row, weigh):
        sums, last_fields, last_weights = [], [], []
        for r in (row, row + 1):
            fields, weights = [], []
            for i in range(PER_ROW):
                code = row_table[0, r * PER_ROW + i]
                fields.append(weigh(x_col, code & 63, col_tiles))
                weights.append(tiles[code >> 6])
            sums.append(wide_dot(jnp.concatenate(fields[:-1], axis=1), weights[:-1]))
            last_fields.append(fields[-1])
            last_weights.append(weights[-1])
        zeros = jnp.zeros_like(last_fields[0])
        lines = jnp.concatenate([
            jnp.concatenate([last_fields[0], zeros], axis=1),
            jnp.concatenate([zeros, last_fields[1]], axis=1)], axis=0)
        last = wide_dot(lines, last_weights)
        height = zeros.shape[0]
        return [sums[0] + last[:height], sums[1] + last[height:]]

    def backward_tiles(col, weigh):
        return [backward_tile(col, weigh), backward_tile(col + 1, weigh)]

    def backward_tile(col, weigh):
        fields, weights = [], []
        for i in range(per_col):
            code = col_table[0, col * per_col + i]
            fields.append(weigh(x_row, code & 127, row_tiles))
            weights.append(tiles[code >> 7])
        return jnp.dot(
            jnp.concatenate(fields, axis=1), jnp.concatenate(weights, axis=0),
            preferred_element_type=jnp.float32)

    def field_of(x_ref, index, limit):
        return x_ref[index]

    def field_and_ones(x_ref, index, limit):
        unit = ones[jnp.where(index == limit, 1, 0)]
        return jnp.concatenate([x_ref[index], unit], axis=0)

    start_gather()
    live = count[0, 0]
    row_codes[...] = slot_table(rows[...], cols[...], live, PER_ROW, 6, col_tiles)
    col_codes[...] = slot_table(cols[...], rows[...], live, per_col, 7, row_tiles)
    table_copies = (
        pltpu.make_async_copy(row_codes, row_table, table_sem.at[0]),
        pltpu.make_async_copy(col_codes, col_table, table_sem.at[1]),
    )
    for copy in table_copies:
        copy.start()
    for i in range(tile_sem.shape[0]):
        tile_copy(i).wait()

    for copy in table_copies:
        copy.wait()

    def chunk_products(j, tiles_of, part, first, d_part):
        for t in range(0, own_tiles, 2):
            products = tiles_of(j * own_tiles + t, field_and_ones if first else field_of)
            for i, product in enumerate(products):
                part[j * own_tiles + t + i] = product[:tasks].astype(part.dtype)
                if first:
                    d_part[j, t + i : t + i + 1, :] = product[tasks : tasks + 1]
        if first:
            d_part[j, own_tiles:, :] = jnp.zeros((8 - own_tiles, 128), jnp.float32)

    def forward_products(first):
        def four(i, carry):
            turn = [4 * i + n for n in range(4)]
            for k in turn:
                chunk_products(partner(me_c, k, n_col), forward_tiles, f_part, first, df_part)
            for k in turn:

                @pl.when(k != own_turn(n_col))
                def _(k=k):
                    j = partner(me_c, k, n_col)
                    f_send(j, me_c).start()
                    if first:
                        df_send(j, me_c).start()
            return carry

        lax.fori_loop(0, n_col // 4, four, 0)

    turns = far_first + [0]
    ahead = [(d, 0) for d in turns]
    behind = [(d, 1) for d in turns]
    order = ahead[:-1] + behind[:-1] + [ahead[-1], behind[-1]]

    def backward_products(first):
        def turn(k):
            d = pick(k, [d for d, final in order])
            final = pick(k, [final for d, final in order])
            return d, final, at_chip(d, core + (1 - final) * (1 - 2 * core))

        def two(i, carry):
            for k in (2 * i, 2 * i + 1):
                d, final, j = turn(k)
                chunk_products(j, backward_tiles, b_part, first, db_part)
            for k in (2 * i, 2 * i + 1):
                d, final, j = turn(k)

                @pl.when(final == 0)
                def _(d=d):
                    pair_copy(d).start()

                @pl.when(final == 1)
                def _(d=d, j=j):
                    pair_copy(d).wait_recv()
                    for t in range(own_tiles):
                        b_part[j * own_tiles + t] = b_part[j * own_tiles + t] + pair[d, t]

                    @pl.when(d != 0)
                    def _():
                        b_send(d).start()

                if first:

                    @pl.when(j != me_r)
                    def _(j=j):
                        db_send(j, me_r).start()
            return carry

        lax.fori_loop(0, n_row // 2, two, 0)

    def gather_sums(n, own, send, recv, totals):
        def one(k, sums):
            j = (own + 1 + k) & (n - 1)
            send(j, j).wait_recv()
            return tuple(s + recv[j, t].astype(jnp.float32) for t, s in enumerate(sums))

        return lax.fori_loop(0, n - 1, one, totals)

    lane = lax.broadcasted_iota(jnp.int32, (tasks, 128), 1)
    task = lax.broadcasted_iota(jnp.int32, (tasks, 128), 0)

    def one_step(step, first):
        pass_on()
        forward_products(first)
        second_phase.wait_recv()
        backward_products(first)
        end_gather_sends()

        if first:
            df_recv[me_c] = df_part[me_c]
            db_recv[me_r] = db_part[me_r]
            all_df.wait_recv()
            all_db.wait_recv()
            total = sum(df_recv[i] for i in range(n_col)) + sum(db_recv[i] for i in range(n_row))
            degree[...] = 0.5 * total

        totals = tuple(
            f_part[me_c * own_tiles + t].astype(jnp.float32)
            + b_part[me_r * own_tiles + t].astype(jnp.float32)
            for t in range(own_tiles))
        totals = gather_sums(n_col, me_c, f_send, f_recv, totals)
        for d in reversed(far_first):
            b_arrival(d).wait_recv()
            source = (y + d) & (chips - 1)
            totals = tuple(s + b_recv[source, t] for t, s in enumerate(totals))

        pq = jnp.zeros((tasks, 128), jnp.float32)
        rq, qq, rr = pq, pq, pq
        images = []
        for t in range(own_tiles):
            part = slice(128 * t, 128 * (t + 1))
            p, r = dir_ref[:, part], res[:, part]
            q = p + coupling * (degree[t : t + 1, :] * p - 0.5 * totals[t])
            images.append(q)
            pq, rq, qq, rr = pq + p * q, rq + r * q, qq + q * q, rr + r * r
        row = jnp.zeros((tasks, 128), jnp.float32)
        for i, s in enumerate((pq, rq, qq, rr)):
            row = jnp.where(lane == task + tasks * i, jnp.sum(s, axis=1, keepdims=True), row)
        row = jnp.sum(row, axis=0, keepdims=True)
        dots_row[me_r] = row
        for k in range(n_row):
            if k != own_turn(n_row):
                d1_copy(partner(me_r, k, n_row), me_r).start()
        all_d1.wait_recv()
        dots_col[me_c] = sum(dots_row[i] for i in range(n_row))
        for k in range(n_col):
            if k != own_turn(n_col):
                d2_copy(partner(me_c, k, n_col), me_c).start()
        all_d2.wait_recv()
        sums = jnp.broadcast_to(sum(dots_col[i] for i in range(n_col)), (tasks, 128))
        pq, rq, qq, rr = (
            jnp.sum(jnp.where(lane == task + tasks * i, sums, 0.0), axis=1, keepdims=True)
            for i in range(4))
        size = rr / pq
        new = jnp.maximum(rr - 2.0 * size * rq + size * size * qq, 0.0)
        ratio = new / rr
        moves = []
        for t in range(own_tiles):
            part = slice(128 * t, 128 * (t + 1))
            p = dir_ref[:, part]
            r = res[:, part] - size * images[t]
            moves.append(size * p)
            res[:, part] = r
            dir_ref[:, part] = r + ratio * p

        @pl.when(step + 1 < ITERS)
        def _():
            start_gather()

        for t in range(own_tiles):
            part = slice(128 * t, 128 * (t + 1))
            sol[:, part] = sol[:, part] + moves[t]
        all_f.wait_send()
        for d in range(chips):
            pair_copy(d).wait_send()
        for d in far_first:
            b_send(d).wait_send()
        all_d1.wait_send()
        all_d2.wait_send()
        if first:
            all_df.wait_send()
            all_db.wait_send()

    one_step(0, True)

    def later_step(step, carry):
        one_step(step, False)
        return carry

    lax.fori_loop(1, ITERS, later_step, 0)


def per_device(n_row, n_col, scores, tile_values, tile_rows, tile_cols, tile_count):
    tiles = tile_values[0, 0]
    rows, cols = tile_rows[0], tile_cols[0]
    slots = tiles.shape[0]
    tasks, piece = scores.shape
    own_tiles = piece // 128
    row_tiles, col_tiles = own_tiles * n_col, own_tiles * n_row
    per_col = slots // col_tiles
    f32 = jnp.float32
    dma = pltpu.SemaphoreType.DMA
    vmem = pl.BlockSpec(memory_space=pltpu.VMEM)
    smem = pl.BlockSpec(memory_space=pltpu.SMEM)
    sol, res = pl.pallas_call(
        functools.partial(cg_kernel, n_row, n_col, per_col),
        out_shape=(
            jax.ShapeDtypeStruct((tasks, piece), f32),
            jax.ShapeDtypeStruct((tasks, piece), f32),
        ),
        in_specs=[smem, vmem, vmem, vmem, pl.BlockSpec(memory_space=pl.ANY)],
        out_specs=(vmem, vmem),
        scratch_shapes=[
            pltpu.VMEM((slots, 128, 128), jnp.bfloat16),
            pltpu.VMEM((col_tiles + 1, tasks, 128), jnp.bfloat16),
            pltpu.VMEM((row_tiles + 1, tasks, 128), jnp.bfloat16),
            pltpu.VMEM((row_tiles, tasks, 128), F_TYPE),
            pltpu.VMEM((col_tiles, tasks, 128), B_TYPE),
            pltpu.VMEM((n_col, own_tiles, tasks, 128), F_TYPE),
            pltpu.VMEM((n_row // 2, own_tiles, tasks, 128), B_TYPE),
            pltpu.VMEM((n_row // 2, own_tiles, tasks, 128), B_TYPE),
            pltpu.VMEM((n_col, 8, 128), f32),
            pltpu.VMEM((n_row, 8, 128), f32),
            pltpu.VMEM((n_col, 8, 128), f32),
            pltpu.VMEM((n_row, 8, 128), f32),
            pltpu.VMEM((2, 16, 128), jnp.bfloat16),
            pltpu.VMEM((tasks, piece), f32),
            pltpu.VMEM((8, 128), f32),
            pltpu.VMEM((n_row, 1, 128), f32),
            pltpu.VMEM((n_col, 1, 128), f32),
            pltpu.VMEM((1, slots), jnp.int32),
            pltpu.VMEM((1, slots), jnp.int32),
            pltpu.SMEM((1, slots), jnp.int32),
            pltpu.SMEM((1, slots), jnp.int32),
            dma((8,)), dma((2,)),
            dma((n_row,)), dma((n_row,)), dma((1,)), dma((1,)),
            dma((spread(n_col)[0],)), dma((spread(n_col)[1],)),
            dma((1,)), dma((n_col,)), dma((n_row // 2,)), dma((n_row // 2,)),
            dma((n_row // 2,)), dma((n_row // 2,)),
            dma((1,)), dma((1,)), dma((1,)), dma((1,)),
            dma((1,)), dma((1,)), dma((1,)), dma((1,)),
        ],
        compiler_params=pltpu.CompilerParams(
            collective_id=0, has_side_effects=True, vmem_limit_bytes=56 * 1024 * 1024
        ),
    )(tile_count, rows, cols, scores, tiles)
    return pl.pallas_call(
        copy_kernel,
        out_shape=(
            jax.ShapeDtypeStruct((tasks, piece), f32),
            jax.ShapeDtypeStruct((tasks, piece), f32),
        ),
        in_specs=[vmem, vmem],
        out_specs=(vmem, vmem),
    )(sol, res)


def solution(mesh):
    return jax.shard_map(
        functools.partial(per_device, mesh.shape["row"], mesh.shape["col"]),
        mesh=mesh,
        in_specs=(
            P(None, ("row", "col")),
            P("row", "col", None, None, None),
            P("row", "col", None),
            P("row", "col", None),
            P("row", "col"),
        ),
        out_specs=(P(None, ("row", "col")), P(None, ("row", "col"))),
        check_vma=False,
    )
```

```python
import functools

import jax
import jax.numpy as jnp
from jax import lax
from jax.experimental import pallas as pl
from jax.experimental.pallas import tpu as pltpu
from jax.sharding import PartitionSpec as P

PER_ROW = 5
ITERS = 3
MESH = pl.DeviceIdType.MESH
F_TYPE = jnp.bfloat16
B_TYPE = jnp.float32

coupling = 0.2


def spread(n):
    fast = 2 if n <= 8 else 4
    return n // fast, fast


def partner(me, k, n):
    slow, fast = spread(n)
    bits = fast.bit_length() - 1
    a = ((me >> bits) + slow // 2 + (k >> bits)) & (slow - 1)
    b = (me + fast // 2 + k) & (fast - 1)
    return a * fast + b


def own_turn(n):
    slow, fast = spread(n)
    return (slow - slow // 2) % slow * fast + (fast - fast // 2) % fast


def slot_table(own, other, live, per_tile, shift, empty):
    n = own.shape[1]
    here = lax.broadcasted_iota(jnp.int32, (n, n), 0)
    there = lax.broadcasted_iota(jnp.int32, (n, n), 1)

    def down(line):
        return jnp.sum(jnp.where(here == there, line, 0), axis=1, keepdims=True)

    own_down, other_down = down(own), down(other)
    earlier = (own_down == own) & (there < here)
    key = own_down * per_tile + jnp.sum(jnp.where(earlier, 1, 0), axis=1, keepdims=True)
    slot = here[:, :1]
    code = (slot << shift) + jnp.where(slot < live, other_down, empty)
    return jnp.sum(jnp.where(key == there, code, 0), axis=0, keepdims=True)


def copy_kernel(sol_in, res_in, sol, res):
    sol[...] = sol_in[...]
    res[...] = res_in[...]


def pick(index, values):
    value = values[-1]
    for i, v in enumerate(values[:-1]):
        value = jnp.where(index == i, v, value)
    return value


def cg_kernel(
    n_row, n_col, per_col,
    count, rows, cols, scores, tiles_hbm, sol, res,
    tiles, x_col, x_row, f_part, b_part, f_recv, b_recv, pair,
    df_part, db_part, df_recv, db_recv, ones, dir_ref, degree, dots_row, dots_col,
    row_codes, col_codes, row_table, col_table,
    tile_sem, table_sem,
    agr_send, agr_recv, agc_send, agc_recv, first_x, first_z,
    rsf_send, rsf_recv, rsb_send, rsb_recv, pair_send, pair_recv,
    dgf_send, dgf_recv, dgb_send, dgb_recv,
    d1_send, d1_recv, d2_send, d2_recv,
):
    me_r = lax.axis_index("row")
    me_c = lax.axis_index("col")
    y, core = me_r >> 1, me_r & 1
    chips = n_row // 2
    sibling = me_r + 1 - 2 * core
    side_x, side_z = spread(n_col)
    x, z = me_c // side_z, me_c % side_z

    def by_distance(side):
        return sorted(range(1, side), key=lambda d: -min(d, side - d))

    far_first, far_x, far_z = by_distance(chips), by_distance(side_x), by_distance(side_z)
    tasks = scores.shape[0]
    own_tiles = scores.shape[1] // 128
    half = own_tiles // 2
    slots = tiles.shape[0]
    col_tiles = b_part.shape[0]
    row_tiles = f_part.shape[0]
    chunk = slots // tile_sem.shape[0]

    def tile_copy(i):
        part = pl.ds(i * chunk, chunk)
        return pltpu.make_async_copy(tiles_hbm.at[part], tiles.at[part], tile_sem.at[i])

    for i in range(tile_sem.shape[0]):
        tile_copy(i).start()

    barrier = pltpu.get_barrier_semaphore()

    def greet(axis, n, own):
        def one(k, carry):
            @pl.when(k != own_turn(n))
            def _():
                j = partner(own, k, n)
                target = (me_r, j) if axis == "col" else (j, me_c)
                pl.semaphore_signal(barrier, inc=1, device_id=target, device_id_type=MESH)
            return carry

        lax.fori_loop(0, n, one, 0)

    greet("col", n_col, me_c)
    greet("row", n_row, me_r)

    x_col[col_tiles] = jnp.zeros((tasks, 128), jnp.bfloat16)
    x_row[row_tiles] = jnp.zeros((tasks, 128), jnp.bfloat16)
    ones[0] = jnp.ones((16, 128), jnp.bfloat16)
    ones[1] = jnp.zeros((16, 128), jnp.bfloat16)
    dir_ref[...] = scores[...]
    res[...] = scores[...]
    sol[...] = jnp.zeros_like(sol)

    pl.semaphore_wait(barrier, n_row + n_col - 2)

    def each_partner(n, own, action):
        def one(k, carry):
            @pl.when(k != own_turn(n))
            def _():
                action(partner(own, k, n))
            return carry

        lax.fori_loop(0, n, one, 0)

    own_col = pl.ds(me_r * own_tiles, own_tiles)
    own_row = pl.ds(me_c * own_tiles, own_tiles)

    def gather_row(j, source, sem):
        part = pl.ds(source * own_tiles, own_tiles)
        return pltpu.make_async_remote_copy(
            src_ref=x_col.at[part], dst_ref=x_col.at[part],
            send_sem=agr_send.at[sem], recv_sem=agr_recv.at[source],
            device_id=(j, me_c), device_id_type=MESH,
        )

    def all_of(ref, number, send_sem, recv_sem):
        part = ref.at[pl.ds(0, number)]
        return pltpu.make_async_remote_copy(
            src_ref=part, dst_ref=part, send_sem=send_sem.at[0], recv_sem=recv_sem.at[0],
            device_id=(sibling, me_c), device_id_type=MESH,
        )

    others_row, others_col = n_row - 1, n_col - 1
    all_cols = all_of(x_row, others_col * own_tiles, agc_send, agc_send)
    second = half * (side_x * (side_z - 1) + side_z * (side_x - 1))
    second_phase = all_of(x_row, second, agc_recv, agc_recv)
    all_f = all_of(f_part, others_col * own_tiles, rsf_send, rsf_send)
    all_df = all_of(df_recv, others_col, dgf_send, dgf_recv)
    all_db = all_of(db_recv, others_row, dgb_send, dgb_recv)
    all_d1 = all_of(dots_row, others_row, d1_send, d1_recv)
    all_d2 = all_of(dots_col, others_col, d2_send, d2_recv)

    def at_chip(d, on_core):
        return ((y + d) & (chips - 1)) * 2 + on_core

    def at_place(dx, dz):
        return ((x + dx) & (side_x - 1)) * side_z + ((z + dz) & (side_z - 1))

    def gather_half(target, source, which, recv_sem):
        part = pl.ds(source * own_tiles + which * half, half)
        return pltpu.make_async_remote_copy(
            src_ref=x_row.at[part], dst_ref=x_row.at[part],
            send_sem=agc_send.at[0], recv_sem=recv_sem,
            device_id=(me_r, target), device_id_type=MESH,
        )

    def start_cols():
        for d in far_x:
            gather_half(at_place(d, 0), me_c, 0, first_x.at[x]).start()
        for d in far_z:
            gather_half(at_place(0, d), me_c, 1, first_z.at[z]).start()
        pass_x_on(0)
        pass_z_on(0)

    def pass_x_on(dx):
        source = at_place(dx, 0)
        if dx:
            gather_half(source, source, 0, first_x.at[(x + dx) & (side_x - 1)]).wait_recv()
        for d in far_z:
            gather_half(at_place(0, d), source, 0, agc_recv.at[0]).start()

    def pass_z_on(dz):
        source = at_place(0, dz)
        if dz:
            gather_half(source, source, 1, first_z.at[(z + dz) & (side_z - 1)]).wait_recv()
        for d in far_x:
            gather_half(at_place(d, 0), source, 1, agc_recv.at[0]).start()

    def send_pieces(j, source, part, recv, send_sem, recv_sem, axis):
        return pltpu.make_async_remote_copy(
            src_ref=part, dst_ref=recv.at[source],
            send_sem=send_sem.at[0], recv_sem=recv_sem.at[source if recv is f_recv else 0],
            device_id=(me_r, j) if axis == "col" else (j, me_c), device_id_type=MESH,
        )

    def f_send(j, source):
        return send_pieces(
            j, source, f_part.at[pl.ds(j * own_tiles, own_tiles)], f_recv, rsf_send, rsf_recv, "col")

    def b_send(d):
        j = at_chip(d, core)
        return pltpu.make_async_remote_copy(
            src_ref=b_part.at[pl.ds(j * own_tiles, own_tiles)], dst_ref=b_recv.at[y],
            send_sem=rsb_send.at[d], recv_sem=rsb_recv.at[y],
            device_id=(j, me_c), device_id_type=MESH,
        )

    def b_arrival(d):
        source = (y + d) & (chips - 1)
        return pltpu.make_async_remote_copy(
            src_ref=b_part.at[pl.ds(me_r * own_tiles, own_tiles)], dst_ref=b_recv.at[source],
            send_sem=rsb_send.at[d], recv_sem=rsb_recv.at[source],
            device_id=(at_chip(d, core), me_c), device_id_type=MESH,
        )

    def pair_copy(d):
        j = at_chip(d, 1 - core)
        return pltpu.make_async_remote_copy(
            src_ref=b_part.at[pl.ds(j * own_tiles, own_tiles)], dst_ref=pair.at[d],
            send_sem=pair_send.at[d], recv_sem=pair_recv.at[d],
            device_id=(sibling, me_c), device_id_type=MESH,
        )

    def df_send(j, source):
        return send_pieces(j, source, df_part.at[j], df_recv, dgf_send, dgf_recv, "col")

    def db_send(j, source):
        return send_pieces(j, source, db_part.at[j], db_recv, dgb_send, dgb_recv, "row")

    def d1_copy(j, source):
        return send_pieces(j, source, dots_row.at[me_r], dots_row, d1_send, d1_recv, "row")

    def d2_copy(j, source):
        return send_pieces(j, source, dots_col.at[me_c], dots_col, d2_send, d2_recv, "col")

    def start_gather():
        for t in range(own_tiles):
            piece = dir_ref[:, 128 * t : 128 * (t + 1)].astype(jnp.bfloat16)
            x_col[me_r * own_tiles + t] = piece
            x_row[me_c * own_tiles + t] = piece
        for d in far_first:
            gather_row(at_chip(d, core), me_r, at_chip(d, core)).start()
        gather_row(sibling, me_r, sibling).start()
        start_cols()

    def pass_y_on(d):
        source = at_chip(d, core)
        gather_row(source, source, source).wait_recv()
        gather_row(sibling, source, at_chip(d, 1 - core)).start()

    def pass_on():
        for d in reversed(far_first[1:]):
            pass_y_on(d)
        for d in reversed(far_x[1:]):
            pass_x_on(d)
        for d in reversed(far_z[1:]):
            pass_z_on(d)
        pass_y_on(far_first[0])
        pass_x_on(far_x[0])
        pass_z_on(far_z[0])
        gather_row(sibling, sibling, sibling).wait_recv()
        for d in reversed(far_first):
            source = at_chip(d, 1 - core)
            gather_row(sibling, source, source).wait_recv()

    def end_gather_sends():
        for d in far_first:
            gather_row(at_chip(d, core), me_r, at_chip(d, core)).wait_send()
            gather_row(sibling, at_chip(d, core), at_chip(d, 1 - core)).wait_send()
        gather_row(sibling, me_r, sibling).wait_send()
        all_cols.wait_send()

    def wide_dot(fields, weights):
        return lax.dot_general(
            fields, jnp.concatenate(weights, axis=1),
            (((1,), (1,)), ((), ())), preferred_element_type=jnp.float32)

    def forward_tiles(row, weigh):
        sums, last_fields, last_weights = [], [], []
        for r in (row, row + 1):
            fields, weights = [], []
            for i in range(PER_ROW):
                code = row_table[0, r * PER_ROW + i]
                fields.append(weigh(x_col, code & 63, col_tiles))
                weights.append(tiles[code >> 6])
            sums.append(wide_dot(jnp.concatenate(fields[:-1], axis=1), weights[:-1]))
            last_fields.append(fields[-1])
            last_weights.append(weights[-1])
        zeros = jnp.zeros_like(last_fields[0])
        lines = jnp.concatenate([
            jnp.concatenate([last_fields[0], zeros], axis=1),
            jnp.concatenate([zeros, last_fields[1]], axis=1)], axis=0)
        last = wide_dot(lines, last_weights)
        height = zeros.shape[0]
        return [sums[0] + last[:height], sums[1] + last[height:]]

    def backward_tiles(col, weigh):
        return [backward_tile(col, weigh), backward_tile(col + 1, weigh)]

    def backward_tile(col, weigh):
        fields, weights = [], []
        for i in range(per_col):
            code = col_table[0, col * per_col + i]
            fields.append(weigh(x_row, code & 127, row_tiles))
            weights.append(tiles[code >> 7])
        return jnp.dot(
            jnp.concatenate(fields, axis=1), jnp.concatenate(weights, axis=0),
            preferred_element_type=jnp.float32)

    def field_of(x_ref, index, limit):
        return x_ref[index]

    def field_and_ones(x_ref, index, limit):
        unit = ones[jnp.where(index == limit, 1, 0)]
        return jnp.concatenate([x_ref[index], unit], axis=0)

    start_gather()
    live = count[0, 0]
    row_codes[...] = slot_table(rows[...], cols[...], live, PER_ROW, 6, col_tiles)
    col_codes[...] = slot_table(cols[...], rows[...], live, per_col, 7, row_tiles)
    table_copies = (
        pltpu.make_async_copy(row_codes, row_table, table_sem.at[0]),
        pltpu.make_async_copy(col_codes, col_table, table_sem.at[1]),
    )
    for copy in table_copies:
        copy.start()
    for i in range(tile_sem.shape[0]):
        tile_copy(i).wait()

    for copy in table_copies:
        copy.wait()

    def chunk_products(j, tiles_of, part, first, d_part):
        for t in range(0, own_tiles, 2):
            products = tiles_of(j * own_tiles + t, field_and_ones if first else field_of)
            for i, product in enumerate(products):
                part[j * own_tiles + t + i] = product[:tasks].astype(part.dtype)
                if first:
                    d_part[j, t + i : t + i + 1, :] = product[tasks : tasks + 1]
        if first:
            d_part[j, own_tiles:, :] = jnp.zeros((8 - own_tiles, 128), jnp.float32)

    def forward_products(first):
        def four(i, carry):
            turn = [4 * i + n for n in range(4)]
            for k in turn:
                chunk_products(partner(me_c, k, n_col), forward_tiles, f_part, first, df_part)
            for k in turn:

                @pl.when(k != own_turn(n_col))
                def _(k=k):
                    j = partner(me_c, k, n_col)
                    f_send(j, me_c).start()
                    if first:
                        df_send(j, me_c).start()
            return carry

        lax.fori_loop(0, n_col // 4, four, 0)

    turns = far_first + [0]
    ahead = [(d, 0) for d in turns]
    behind = [(d, 1) for d in turns]
    order = ahead[:-1] + behind[:-1] + [ahead[-1], behind[-1]]

    def backward_products(first):
        def turn(k):
            d = pick(k, [d for d, final in order])
            final = pick(k, [final for d, final in order])
            return d, final, at_chip(d, core + (1 - final) * (1 - 2 * core))

        def two(i, carry):
            for k in (2 * i, 2 * i + 1):
                d, final, j = turn(k)
                chunk_products(j, backward_tiles, b_part, first, db_part)
            for k in (2 * i, 2 * i + 1):
                d, final, j = turn(k)

                @pl.when(final == 0)
                def _(d=d):
                    pair_copy(d).start()

                @pl.when(final == 1)
                def _(d=d, j=j):
                    pair_copy(d).wait_recv()
                    for t in range(own_tiles):
                        b_part[j * own_tiles + t] = b_part[j * own_tiles + t] + pair[d, t]

                    @pl.when(d != 0)
                    def _():
                        b_send(d).start()

                if first:

                    @pl.when(j != me_r)
                    def _(j=j):
                        db_send(j, me_r).start()
            return carry

        lax.fori_loop(0, n_row // 2, two, 0)

    def gather_sums(n, own, send, recv, totals):
        def one(k, sums):
            j = (own + 1 + k) & (n - 1)
            send(j, j).wait_recv()
            return tuple(s + recv[j, t].astype(jnp.float32) for t, s in enumerate(sums))

        return lax.fori_loop(0, n - 1, one, totals)

    lane = lax.broadcasted_iota(jnp.int32, (tasks, 128), 1)
    task = lax.broadcasted_iota(jnp.int32, (tasks, 128), 0)

    def one_step(step, first):
        pass_on()
        forward_products(first)
        second_phase.wait_recv()
        backward_products(first)
        end_gather_sends()

        if first:
            df_recv[me_c] = df_part[me_c]
            db_recv[me_r] = db_part[me_r]
            all_df.wait_recv()
            all_db.wait_recv()
            total = sum(df_recv[i] for i in range(n_col)) + sum(db_recv[i] for i in range(n_row))
            degree[...] = 0.5 * total

        totals = tuple(
            f_part[me_c * own_tiles + t].astype(jnp.float32)
            + b_part[me_r * own_tiles + t].astype(jnp.float32)
            for t in range(own_tiles))
        totals = gather_sums(n_col, me_c, f_send, f_recv, totals)
        for d in reversed(far_first):
            b_arrival(d).wait_recv()
            source = (y + d) & (chips - 1)
            totals = tuple(s + b_recv[source, t] for t, s in enumerate(totals))

        pq = jnp.zeros((tasks, 128), jnp.float32)
        rq, qq, rr = pq, pq, pq
        images = []
        for t in range(own_tiles):
            part = slice(128 * t, 128 * (t + 1))
            p, r = dir_ref[:, part], res[:, part]
            q = p + coupling * (degree[t : t + 1, :] * p - 0.5 * totals[t])
            images.append(q)
            pq, rq, qq, rr = pq + p * q, rq + r * q, qq + q * q, rr + r * r
        row = jnp.zeros((tasks, 128), jnp.float32)
        for i, s in enumerate((pq, rq, qq, rr)):
            row = jnp.where(lane == task + tasks * i, jnp.sum(s, axis=1, keepdims=True), row)
        row = jnp.sum(row, axis=0, keepdims=True)
        dots_row[me_r] = row
        for k in range(n_row):
            if k != own_turn(n_row):
                d1_copy(partner(me_r, k, n_row), me_r).start()
        all_d1.wait_recv()
        dots_col[me_c] = sum(dots_row[i] for i in range(n_row))
        for k in range(n_col):
            if k != own_turn(n_col):
                d2_copy(partner(me_c, k, n_col), me_c).start()
        all_d2.wait_recv()
        sums = jnp.broadcast_to(sum(dots_col[i] for i in range(n_col)), (tasks, 128))
        pq, rq, qq, rr = (
            jnp.sum(jnp.where(lane == task + tasks * i, sums, 0.0), axis=1, keepdims=True)
            for i in range(4))
        size = rr / pq
        new = jnp.maximum(rr - 2.0 * size * rq + size * size * qq, 0.0)
        ratio = new / rr
        moves = []
        for t in range(own_tiles):
            part = slice(128 * t, 128 * (t + 1))
            p = dir_ref[:, part]
            r = res[:, part] - size * images[t]
            moves.append(size * p)
            res[:, part] = r
            dir_ref[:, part] = r + ratio * p

        @pl.when(step + 1 < ITERS)
        def _():
            start_gather()

        for t in range(own_tiles):
            part = slice(128 * t, 128 * (t + 1))
            sol[:, part] = sol[:, part] + moves[t]
        all_f.wait_send()
        for d in range(chips):
            pair_copy(d).wait_send()
        for d in far_first:
            b_send(d).wait_send()
        all_d1.wait_send()
        all_d2.wait_send()
        if first:
            all_df.wait_send()
            all_db.wait_send()

    one_step(0, True)

    def later_step(step, carry):
        one_step(step, False)
        return carry

    lax.fori_loop(1, ITERS, later_step, 0)


def per_device(n_row, n_col, scores, tile_values, tile_rows, tile_cols, tile_count):
    tiles = tile_values[0, 0]
    rows, cols = tile_rows[0], tile_cols[0]
    slots = tiles.shape[0]
    tasks, piece = scores.shape
    own_tiles = piece // 128
    row_tiles, col_tiles = own_tiles * n_col, own_tiles * n_row
    per_col = slots // col_tiles
    f32 = jnp.float32
    dma = pltpu.SemaphoreType.DMA
    vmem = pl.BlockSpec(memory_space=pltpu.VMEM)
    smem = pl.BlockSpec(memory_space=pltpu.SMEM)
    sol, res = pl.pallas_call(
        functools.partial(cg_kernel, n_row, n_col, per_col),
        out_shape=(pltpu.VMEM((tasks, piece), f32), pltpu.VMEM((tasks, piece), f32)),
        in_specs=[smem, vmem, vmem, vmem, pl.BlockSpec(memory_space=pl.ANY)],
        out_specs=(vmem, vmem),
        scratch_shapes=[
            pltpu.VMEM((slots, 128, 128), jnp.bfloat16),
            pltpu.VMEM((col_tiles + 1, tasks, 128), jnp.bfloat16),
            pltpu.VMEM((row_tiles + 1, tasks, 128), jnp.bfloat16),
            pltpu.VMEM((row_tiles, tasks, 128), F_TYPE),
            pltpu.VMEM((col_tiles, tasks, 128), B_TYPE),
            pltpu.VMEM((n_col, own_tiles, tasks, 128), F_TYPE),
            pltpu.VMEM((n_row // 2, own_tiles, tasks, 128), B_TYPE),
            pltpu.VMEM((n_row // 2, own_tiles, tasks, 128), B_TYPE),
            pltpu.VMEM((n_col, 8, 128), f32),
            pltpu.VMEM((n_row, 8, 128), f32),
            pltpu.VMEM((n_col, 8, 128), f32),
            pltpu.VMEM((n_row, 8, 128), f32),
            pltpu.VMEM((2, 16, 128), jnp.bfloat16),
            pltpu.VMEM((tasks, piece), f32),
            pltpu.VMEM((8, 128), f32),
            pltpu.VMEM((n_row, 1, 128), f32),
            pltpu.VMEM((n_col, 1, 128), f32),
            pltpu.VMEM((1, slots), jnp.int32),
            pltpu.VMEM((1, slots), jnp.int32),
            pltpu.SMEM((1, slots), jnp.int32),
            pltpu.SMEM((1, slots), jnp.int32),
            dma((8,)), dma((2,)),
            dma((n_row,)), dma((n_row,)), dma((1,)), dma((1,)),
            dma((spread(n_col)[0],)), dma((spread(n_col)[1],)),
            dma((1,)), dma((n_col,)), dma((n_row // 2,)), dma((n_row // 2,)),
            dma((n_row // 2,)), dma((n_row // 2,)),
            dma((1,)), dma((1,)), dma((1,)), dma((1,)),
            dma((1,)), dma((1,)), dma((1,)), dma((1,)),
        ],
        compiler_params=pltpu.CompilerParams(
            collective_id=0, has_side_effects=True, vmem_limit_bytes=56 * 1024 * 1024
        ),
    )(tile_count, rows, cols, scores, tiles)
    return pl.pallas_call(
        copy_kernel,
        out_shape=(
            jax.ShapeDtypeStruct((tasks, piece), f32),
            jax.ShapeDtypeStruct((tasks, piece), f32),
        ),
        in_specs=[vmem, vmem],
        out_specs=(vmem, vmem),
    )(
        pltpu.with_memory_space_constraint(sol, pltpu.VMEM),
        pltpu.with_memory_space_constraint(res, pltpu.VMEM),
    )


def solution(mesh):
    return jax.shard_map(
        functools.partial(per_device, mesh.shape["row"], mesh.shape["col"]),
        mesh=mesh,
        in_specs=(
            P(None, ("row", "col")),
            P("row", "col", None, None, None),
            P("row", "col", None),
            P("row", "col", None),
            P("row", "col"),
        ),
        out_specs=(P(None, ("row", "col")), P(None, ("row", "col"))),
        check_vma=False,
    )
```

```python
import functools

import jax
import jax.numpy as jnp
from jax import lax
from jax.experimental import pallas as pl
from jax.experimental.pallas import tpu as pltpu
from jax.sharding import PartitionSpec as P

PER_ROW = 5
ITERS = 3
MESH = pl.DeviceIdType.MESH
F_TYPE = jnp.bfloat16
B_TYPE = jnp.float32

coupling = 0.2


def spread(n):
    fast = 2 if n <= 8 else 4
    return n // fast, fast


def partner(me, k, n):
    slow, fast = spread(n)
    bits = fast.bit_length() - 1
    a = ((me >> bits) + slow // 2 + (k >> bits)) & (slow - 1)
    b = (me + fast // 2 + k) & (fast - 1)
    return a * fast + b


def own_turn(n):
    slow, fast = spread(n)
    return (slow - slow // 2) % slow * fast + (fast - fast // 2) % fast


def slot_table(own, other, live, per_tile, shift, empty):
    n = own.shape[1]
    here = lax.broadcasted_iota(jnp.int32, (n, n), 0)
    there = lax.broadcasted_iota(jnp.int32, (n, n), 1)

    def down(line):
        return jnp.sum(jnp.where(here == there, line, 0), axis=1, keepdims=True)

    own_down, other_down = down(own), down(other)
    earlier = (own_down == own) & (there < here)
    key = own_down * per_tile + jnp.sum(jnp.where(earlier, 1, 0), axis=1, keepdims=True)
    slot = here[:, :1]
    code = (slot << shift) + jnp.where(slot < live, other_down, empty)
    return jnp.sum(jnp.where(key == there, code, 0), axis=0, keepdims=True)


def copy_kernel(sol_in, res_in, sol, res):
    sol[...] = sol_in[...]
    res[...] = res_in[...]


def pick(index, values):
    value = values[-1]
    for i, v in enumerate(values[:-1]):
        value = jnp.where(index == i, v, value)
    return value


def cg_kernel(
    n_row, n_col, per_col,
    count, rows, cols, scores, tiles_hbm, sol, res,
    tiles, x_col, x_row, f_part, b_part, f_recv, b_recv, pair,
    df_part, db_part, df_recv, db_recv, ones, dir_ref, degree, dots_row, dots_col,
    row_codes, col_codes, row_table, col_table,
    tile_sem, table_sem,
    agr_send, agr_recv, agc_send, agc_recv, first_x, first_z,
    rsf_send, rsf_recv, rsb_send, rsb_recv, pair_send, pair_recv,
    dgf_send, dgf_recv, dgb_send, dgb_recv,
    d1_send, d1_recv, d2_send, d2_recv,
):
    me_r = lax.axis_index("row")
    me_c = lax.axis_index("col")
    y, core = me_r >> 1, me_r & 1
    chips = n_row // 2
    sibling = me_r + 1 - 2 * core
    side_x, side_z = spread(n_col)
    x, z = me_c // side_z, me_c % side_z

    def by_distance(side):
        return sorted(range(1, side), key=lambda d: -min(d, side - d))

    far_first, far_x, far_z = by_distance(chips), by_distance(side_x), by_distance(side_z)
    tasks = scores.shape[0]
    own_tiles = scores.shape[1] // 128
    half = own_tiles // 2
    slots = tiles.shape[0]
    col_tiles = b_part.shape[0]
    row_tiles = f_part.shape[0]
    chunk = slots // tile_sem.shape[0]

    def tile_copy(i):
        part = pl.ds(i * chunk, chunk)
        return pltpu.make_async_copy(tiles_hbm.at[part], tiles.at[part], tile_sem.at[i])

    for i in range(tile_sem.shape[0]):
        tile_copy(i).start()

    barrier = pltpu.get_barrier_semaphore()

    def greet(axis, n, own):
        def one(k, carry):
            @pl.when(k != own_turn(n))
            def _():
                j = partner(own, k, n)
                target = (me_r, j) if axis == "col" else (j, me_c)
                pl.semaphore_signal(barrier, inc=1, device_id=target, device_id_type=MESH)
            return carry

        lax.fori_loop(0, n, one, 0)

    greet("col", n_col, me_c)
    greet("row", n_row, me_r)

    x_col[col_tiles] = jnp.zeros((tasks, 128), jnp.bfloat16)
    x_row[row_tiles] = jnp.zeros((tasks, 128), jnp.bfloat16)
    ones[0] = jnp.ones((16, 128), jnp.bfloat16)
    ones[1] = jnp.zeros((16, 128), jnp.bfloat16)
    dir_ref[...] = scores[...]
    res[...] = scores[...]
    sol[...] = jnp.zeros_like(sol)

    pl.semaphore_wait(barrier, n_row + n_col - 2)

    def each_partner(n, own, action):
        def one(k, carry):
            @pl.when(k != own_turn(n))
            def _():
                action(partner(own, k, n))
            return carry

        lax.fori_loop(0, n, one, 0)

    own_col = pl.ds(me_r * own_tiles, own_tiles)
    own_row = pl.ds(me_c * own_tiles, own_tiles)

    def gather_row(j, source, sem):
        part = pl.ds(source * own_tiles, own_tiles)
        return pltpu.make_async_remote_copy(
            src_ref=x_col.at[part], dst_ref=x_col.at[part],
            send_sem=agr_send.at[sem], recv_sem=agr_recv.at[source],
            device_id=(j, me_c), device_id_type=MESH,
        )

    def all_of(ref, number, send_sem, recv_sem):
        part = ref.at[pl.ds(0, number)]
        return pltpu.make_async_remote_copy(
            src_ref=part, dst_ref=part, send_sem=send_sem.at[0], recv_sem=recv_sem.at[0],
            device_id=(sibling, me_c), device_id_type=MESH,
        )

    others_row, others_col = n_row - 1, n_col - 1
    all_cols = all_of(x_row, others_col * own_tiles, agc_send, agc_send)
    second = half * (side_x * (side_z - 1) + side_z * (side_x - 1))
    second_phase = all_of(x_row, second, agc_recv, agc_recv)
    all_f = all_of(f_part, others_col * own_tiles, rsf_send, rsf_send)
    all_df = all_of(df_recv, others_col, dgf_send, dgf_recv)
    all_db = all_of(db_recv, others_row, dgb_send, dgb_recv)
    all_d1 = all_of(dots_row, others_row, d1_send, d1_recv)
    all_d2 = all_of(dots_col, others_col, d2_send, d2_recv)

    def at_chip(d, on_core):
        return ((y + d) & (chips - 1)) * 2 + on_core

    def at_place(dx, dz):
        return ((x + dx) & (side_x - 1)) * side_z + ((z + dz) & (side_z - 1))

    def gather_half(target, source, which, recv_sem):
        part = pl.ds(source * own_tiles + which * half, half)
        return pltpu.make_async_remote_copy(
            src_ref=x_row.at[part], dst_ref=x_row.at[part],
            send_sem=agc_send.at[0], recv_sem=recv_sem,
            device_id=(me_r, target), device_id_type=MESH,
        )

    def start_cols():
        for d in far_x:
            gather_half(at_place(d, 0), me_c, 0, first_x.at[x]).start()
        for d in far_z:
            gather_half(at_place(0, d), me_c, 1, first_z.at[z]).start()
        pass_x_on(0)
        pass_z_on(0)

    def pass_x_on(dx):
        source = at_place(dx, 0)
        if dx:
            gather_half(source, source, 0, first_x.at[(x + dx) & (side_x - 1)]).wait_recv()
        for d in far_z:
            gather_half(at_place(0, d), source, 0, agc_recv.at[0]).start()

    def pass_z_on(dz):
        source = at_place(0, dz)
        if dz:
            gather_half(source, source, 1, first_z.at[(z + dz) & (side_z - 1)]).wait_recv()
        for d in far_x:
            gather_half(at_place(d, 0), source, 1, agc_recv.at[0]).start()

    def send_pieces(j, source, part, recv, send_sem, recv_sem, axis):
        return pltpu.make_async_remote_copy(
            src_ref=part, dst_ref=recv.at[source],
            send_sem=send_sem.at[0], recv_sem=recv_sem.at[source if recv is f_recv else 0],
            device_id=(me_r, j) if axis == "col" else (j, me_c), device_id_type=MESH,
        )

    def f_send(j, source):
        return send_pieces(
            j, source, f_part.at[pl.ds(j * own_tiles, own_tiles)], f_recv, rsf_send, rsf_recv, "col")

    def b_send(d):
        j = at_chip(d, core)
        return pltpu.make_async_remote_copy(
            src_ref=b_part.at[pl.ds(j * own_tiles, own_tiles)], dst_ref=b_recv.at[y],
            send_sem=rsb_send.at[d], recv_sem=rsb_recv.at[y],
            device_id=(j, me_c), device_id_type=MESH,
        )

    def b_arrival(d):
        source = (y + d) & (chips - 1)
        return pltpu.make_async_remote_copy(
            src_ref=b_part.at[pl.ds(me_r * own_tiles, own_tiles)], dst_ref=b_recv.at[source],
            send_sem=rsb_send.at[d], recv_sem=rsb_recv.at[source],
            device_id=(at_chip(d, core), me_c), device_id_type=MESH,
        )

    def pair_copy(d):
        j = at_chip(d, 1 - core)
        return pltpu.make_async_remote_copy(
            src_ref=b_part.at[pl.ds(j * own_tiles, own_tiles)], dst_ref=pair.at[d],
            send_sem=pair_send.at[d], recv_sem=pair_recv.at[d],
            device_id=(sibling, me_c), device_id_type=MESH,
        )

    def df_send(j, source):
        return send_pieces(j, source, df_part.at[j], df_recv, dgf_send, dgf_recv, "col")

    def db_send(j, source):
        return send_pieces(j, source, db_part.at[j], db_recv, dgb_send, dgb_recv, "row")

    def d1_copy(j, source):
        return send_pieces(j, source, dots_row.at[me_r], dots_row, d1_send, d1_recv, "row")

    def d2_copy(j, source):
        return send_pieces(j, source, dots_col.at[me_c], dots_col, d2_send, d2_recv, "col")

    def start_gather():
        pieces = [
            dir_ref[:, 128 * t : 128 * (t + 1)].astype(jnp.bfloat16) for t in range(own_tiles)]
        for t in range(own_tiles):
            x_col[me_r * own_tiles + t] = pieces[t]
        for d in far_first:
            gather_row(at_chip(d, core), me_r, at_chip(d, core)).start()
        gather_row(sibling, me_r, sibling).start()
        for t in range(own_tiles):
            x_row[me_c * own_tiles + t] = pieces[t]
        start_cols()

    def pass_y_on(d):
        source = at_chip(d, core)
        gather_row(source, source, source).wait_recv()
        gather_row(sibling, source, at_chip(d, 1 - core)).start()

    def pass_on():
        for d in reversed(far_first[1:]):
            pass_y_on(d)
        for d in reversed(far_x[1:]):
            pass_x_on(d)
        for d in reversed(far_z[1:]):
            pass_z_on(d)
        pass_y_on(far_first[0])
        pass_x_on(far_x[0])
        pass_z_on(far_z[0])
        gather_row(sibling, sibling, sibling).wait_recv()
        for d in reversed(far_first):
            source = at_chip(d, 1 - core)
            gather_row(sibling, source, source).wait_recv()

    def end_gather_sends():
        for d in far_first:
            gather_row(at_chip(d, core), me_r, at_chip(d, core)).wait_send()
            gather_row(sibling, at_chip(d, core), at_chip(d, 1 - core)).wait_send()
        gather_row(sibling, me_r, sibling).wait_send()
        all_cols.wait_send()

    def wide_dot(fields, weights):
        return lax.dot_general(
            fields, jnp.concatenate(weights, axis=1),
            (((1,), (1,)), ((), ())), preferred_element_type=jnp.float32)

    def forward_tiles(row, weigh):
        sums, last_fields, last_weights = [], [], []
        for r in (row, row + 1):
            fields, weights = [], []
            for i in range(PER_ROW):
                code = row_table[0, r * PER_ROW + i]
                fields.append(weigh(x_col, code & 63, col_tiles))
                weights.append(tiles[code >> 6])
            sums.append(wide_dot(jnp.concatenate(fields[:-1], axis=1), weights[:-1]))
            last_fields.append(fields[-1])
            last_weights.append(weights[-1])
        zeros = jnp.zeros_like(last_fields[0])
        lines = jnp.concatenate([
            jnp.concatenate([last_fields[0], zeros], axis=1),
            jnp.concatenate([zeros, last_fields[1]], axis=1)], axis=0)
        last = wide_dot(lines, last_weights)
        height = zeros.shape[0]
        return [sums[0] + last[:height], sums[1] + last[height:]]

    def backward_tiles(col, weigh):
        return [backward_tile(col, weigh), backward_tile(col + 1, weigh)]

    def backward_tile(col, weigh):
        fields, weights = [], []
        for i in range(per_col):
            code = col_table[0, col * per_col + i]
            fields.append(weigh(x_row, code & 127, row_tiles))
            weights.append(tiles[code >> 7])
        return jnp.dot(
            jnp.concatenate(fields, axis=1), jnp.concatenate(weights, axis=0),
            preferred_element_type=jnp.float32)

    def field_of(x_ref, index, limit):
        return x_ref[index]

    def field_and_ones(x_ref, index, limit):
        unit = ones[jnp.where(index == limit, 1, 0)]
        return jnp.concatenate([x_ref[index], unit], axis=0)

    start_gather()
    live = count[0, 0]
    row_codes[...] = slot_table(rows[...], cols[...], live, PER_ROW, 6, col_tiles)
    col_codes[...] = slot_table(cols[...], rows[...], live, per_col, 7, row_tiles)
    table_copies = (
        pltpu.make_async_copy(row_codes, row_table, table_sem.at[0]),
        pltpu.make_async_copy(col_codes, col_table, table_sem.at[1]),
    )
    for copy in table_copies:
        copy.start()
    for i in range(tile_sem.shape[0]):
        tile_copy(i).wait()

    for copy in table_copies:
        copy.wait()

    def chunk_products(j, tiles_of, part, first, d_part):
        for t in range(0, own_tiles, 2):
            products = tiles_of(j * own_tiles + t, field_and_ones if first else field_of)
            for i, product in enumerate(products):
                part[j * own_tiles + t + i] = product[:tasks].astype(part.dtype)
                if first:
                    d_part[j, t + i : t + i + 1, :] = product[tasks : tasks + 1]
        if first:
            d_part[j, own_tiles:, :] = jnp.zeros((8 - own_tiles, 128), jnp.float32)

    def forward_products(first):
        def four(i, carry):
            turn = [4 * i + n for n in range(4)]
            for k in turn:
                chunk_products(partner(me_c, k, n_col), forward_tiles, f_part, first, df_part)
            for k in turn:

                @pl.when(k != own_turn(n_col))
                def _(k=k):
                    j = partner(me_c, k, n_col)
                    f_send(j, me_c).start()
                    if first:
                        df_send(j, me_c).start()
            return carry

        lax.fori_loop(0, n_col // 4, four, 0)

    turns = far_first + [0]
    ahead = [(d, 0) for d in turns]
    behind = [(d, 1) for d in turns]
    order = ahead[:-1] + behind[:-1] + [ahead[-1], behind[-1]]

    def backward_products(first):
        def turn(k):
            d = pick(k, [d for d, final in order])
            final = pick(k, [final for d, final in order])
            return d, final, at_chip(d, core + (1 - final) * (1 - 2 * core))

        def two(i, carry):
            for k in (2 * i, 2 * i + 1):
                d, final, j = turn(k)
                chunk_products(j, backward_tiles, b_part, first, db_part)
            for k in (2 * i, 2 * i + 1):
                d, final, j = turn(k)

                @pl.when(final == 0)
                def _(d=d):
                    pair_copy(d).start()

                @pl.when(final == 1)
                def _(d=d, j=j):
                    pair_copy(d).wait_recv()
                    for t in range(own_tiles):
                        b_part[j * own_tiles + t] = b_part[j * own_tiles + t] + pair[d, t]

                    @pl.when(d != 0)
                    def _():
                        b_send(d).start()

                if first:

                    @pl.when(j != me_r)
                    def _(j=j):
                        db_send(j, me_r).start()
            return carry

        lax.fori_loop(0, n_row // 2, two, 0)

    def gather_sums(n, own, send, recv, totals):
        def one(k, sums):
            j = (own + 1 + k) & (n - 1)
            send(j, j).wait_recv()
            return tuple(s + recv[j, t].astype(jnp.float32) for t, s in enumerate(sums))

        return lax.fori_loop(0, n - 1, one, totals)

    lane = lax.broadcasted_iota(jnp.int32, (tasks, 128), 1)
    task = lax.broadcasted_iota(jnp.int32, (tasks, 128), 0)

    def one_step(step, first):
        pass_on()
        forward_products(first)
        second_phase.wait_recv()
        backward_products(first)
        end_gather_sends()

        if first:
            df_recv[me_c] = df_part[me_c]
            db_recv[me_r] = db_part[me_r]
            all_df.wait_recv()
            all_db.wait_recv()
            total = sum(df_recv[i] for i in range(n_col)) + sum(db_recv[i] for i in range(n_row))
            degree[...] = 0.5 * total

        totals = tuple(
            f_part[me_c * own_tiles + t].astype(jnp.float32)
            + b_part[me_r * own_tiles + t].astype(jnp.float32)
            for t in range(own_tiles))
        totals = gather_sums(n_col, me_c, f_send, f_recv, totals)
        for d in reversed(far_first):
            b_arrival(d).wait_recv()
            source = (y + d) & (chips - 1)
            totals = tuple(s + b_recv[source, t] for t, s in enumerate(totals))

        pq = jnp.zeros((tasks, 128), jnp.float32)
        rq, qq, rr = pq, pq, pq
        images = []
        for t in range(own_tiles):
            part = slice(128 * t, 128 * (t + 1))
            p, r = dir_ref[:, part], res[:, part]
            q = p + coupling * (degree[t : t + 1, :] * p - 0.5 * totals[t])
            images.append(q)
            pq, rq, qq, rr = pq + p * q, rq + r * q, qq + q * q, rr + r * r
        row = jnp.zeros((tasks, 128), jnp.float32)
        for i, s in enumerate((pq, rq, qq, rr)):
            row = jnp.where(lane == task + tasks * i, jnp.sum(s, axis=1, keepdims=True), row)
        row = jnp.sum(row, axis=0, keepdims=True)
        dots_row[me_r] = row
        for k in range(n_row):
            if k != own_turn(n_row):
                d1_copy(partner(me_r, k, n_row), me_r).start()
        all_d1.wait_recv()
        dots_col[me_c] = sum(dots_row[i] for i in range(n_row))
        for k in range(n_col):
            if k != own_turn(n_col):
                d2_copy(partner(me_c, k, n_col), me_c).start()
        all_d2.wait_recv()
        sums = jnp.broadcast_to(sum(dots_col[i] for i in range(n_col)), (tasks, 128))
        pq, rq, qq, rr = (
            jnp.sum(jnp.where(lane == task + tasks * i, sums, 0.0), axis=1, keepdims=True)
            for i in range(4))
        size = rr / pq
        new = jnp.maximum(rr - 2.0 * size * rq + size * size * qq, 0.0)
        ratio = new / rr
        moves = []
        for t in range(own_tiles):
            part = slice(128 * t, 128 * (t + 1))
            p = dir_ref[:, part]
            r = res[:, part] - size * images[t]
            moves.append(size * p)
            res[:, part] = r
            dir_ref[:, part] = r + ratio * p

        @pl.when(step + 1 < ITERS)
        def _():
            start_gather()

        for t in range(own_tiles):
            part = slice(128 * t, 128 * (t + 1))
            sol[:, part] = sol[:, part] + moves[t]
        all_f.wait_send()
        for d in range(chips):
            pair_copy(d).wait_send()
        for d in far_first:
            b_send(d).wait_send()
        all_d1.wait_send()
        all_d2.wait_send()
        if first:
            all_df.wait_send()
            all_db.wait_send()

    one_step(0, True)

    def later_step(step, carry):
        one_step(step, False)
        return carry

    lax.fori_loop(1, ITERS, later_step, 0)


def per_device(n_row, n_col, scores, tile_values, tile_rows, tile_cols, tile_count):
    tiles = tile_values[0, 0]
    rows, cols = tile_rows[0], tile_cols[0]
    slots = tiles.shape[0]
    tasks, piece = scores.shape
    own_tiles = piece // 128
    row_tiles, col_tiles = own_tiles * n_col, own_tiles * n_row
    per_col = slots // col_tiles
    f32 = jnp.float32
    dma = pltpu.SemaphoreType.DMA
    vmem = pl.BlockSpec(memory_space=pltpu.VMEM)
    smem = pl.BlockSpec(memory_space=pltpu.SMEM)
    sol, res = pl.pallas_call(
        functools.partial(cg_kernel, n_row, n_col, per_col),
        out_shape=(pltpu.VMEM((tasks, piece), f32), pltpu.VMEM((tasks, piece), f32)),
        in_specs=[smem, vmem, vmem, vmem, pl.BlockSpec(memory_space=pl.ANY)],
        out_specs=(vmem, vmem),
        scratch_shapes=[
            pltpu.VMEM((slots, 128, 128), jnp.bfloat16),
            pltpu.VMEM((col_tiles + 1, tasks, 128), jnp.bfloat16),
            pltpu.VMEM((row_tiles + 1, tasks, 128), jnp.bfloat16),
            pltpu.VMEM((row_tiles, tasks, 128), F_TYPE),
            pltpu.VMEM((col_tiles, tasks, 128), B_TYPE),
            pltpu.VMEM((n_col, own_tiles, tasks, 128), F_TYPE),
            pltpu.VMEM((n_row // 2, own_tiles, tasks, 128), B_TYPE),
            pltpu.VMEM((n_row // 2, own_tiles, tasks, 128), B_TYPE),
            pltpu.VMEM((n_col, 8, 128), f32),
            pltpu.VMEM((n_row, 8, 128), f32),
            pltpu.VMEM((n_col, 8, 128), f32),
            pltpu.VMEM((n_row, 8, 128), f32),
            pltpu.VMEM((2, 16, 128), jnp.bfloat16),
            pltpu.VMEM((tasks, piece), f32),
            pltpu.VMEM((8, 128), f32),
            pltpu.VMEM((n_row, 1, 128), f32),
            pltpu.VMEM((n_col, 1, 128), f32),
            pltpu.VMEM((1, slots), jnp.int32),
            pltpu.VMEM((1, slots), jnp.int32),
            pltpu.SMEM((1, slots), jnp.int32),
            pltpu.SMEM((1, slots), jnp.int32),
            dma((8,)), dma((2,)),
            dma((n_row,)), dma((n_row,)), dma((1,)), dma((1,)),
            dma((spread(n_col)[0],)), dma((spread(n_col)[1],)),
            dma((1,)), dma((n_col,)), dma((n_row // 2,)), dma((n_row // 2,)),
            dma((n_row // 2,)), dma((n_row // 2,)),
            dma((1,)), dma((1,)), dma((1,)), dma((1,)),
            dma((1,)), dma((1,)), dma((1,)), dma((1,)),
        ],
        compiler_params=pltpu.CompilerParams(
            collective_id=0, has_side_effects=True, vmem_limit_bytes=56 * 1024 * 1024
        ),
    )(tile_count, rows, cols, scores, tiles)
    return pl.pallas_call(
        copy_kernel,
        out_shape=(
            jax.ShapeDtypeStruct((tasks, piece), f32),
            jax.ShapeDtypeStruct((tasks, piece), f32),
        ),
        in_specs=[vmem, vmem],
        out_specs=(vmem, vmem),
    )(
        pltpu.with_memory_space_constraint(sol, pltpu.VMEM),
        pltpu.with_memory_space_constraint(res, pltpu.VMEM),
    )


def solution(mesh):
    return jax.shard_map(
        functools.partial(per_device, mesh.shape["row"], mesh.shape["col"]),
        mesh=mesh,
        in_specs=(
            P(None, ("row", "col")),
            P("row", "col", None, None, None),
            P("row", "col", None),
            P("row", "col", None),
            P("row", "col"),
        ),
        out_specs=(P(None, ("row", "col")), P(None, ("row", "col"))),
        check_vma=False,
    )
```
